32 devices in a mesh: lat: 4 (over y, x), lon: 8 (over z, core).
Axes of the slice: x: 2, y: 2, z: 4, core: 2. Of those that a mesh axis runs over, the one named last changes fastest.
Arguments:
- predicted_quantities: bfloat16 [3, 8, 256, 4096], P(None, None, 'lat', 'lon'), may hold values from -60 to 60
- monitor_coefficients: float32 [8], replicated, may hold values from 0.2 to 2
- departing_pieces: int32 [4, 8, 8, 32], P('lat', 'lon'), may hold values from 0 to 255
- departing_occupancy: int32 [4, 8, 8], P('lat', 'lon'), may hold values from 1 to 32, as said below
- arriving_pieces: int32 [4, 8, 8, 32], P('lat', 'lon'), may hold values from 0 to 255
- interpolant_coefficients: bfloat16 [4, 8, 8, 32, 128, 128], P('lat', 'lon'), may hold values from -0.5 to 0.5
Outputs:
- potential: float32 [256, 4096], P('lat', 'lon')
- scaled_residual: float32 [256, 4096], P('lat', 'lon')
The draws below stay inside these ranges and needn't reach their ends.
Inputs may be any that keep to these rules, and one draw needn't show every extreme that they name: `departing_occupancy`: in each lat row a quarter of the lon indices, drawn from the seed, receive 32 tiles from every device of the row; every other count is at most 16.
All inputs are finite; a program needn't handle non-finite values.
Results may differ from the reference program's by a relative error of at most 0.00087.
Values may be sent and summed in bfloat16 or wider, within the bound.
No kernel may reach another device: no remote copies, remote signals or barrier semaphores. Data moves between devices by JAX's collectives and lax.ppermute only.
A program may use at most 64 MiB of HBM per device.

```python
import math
import jax
import jax.numpy as jnp
from jax import lax

FIELDS = 8
TILE = 128
CAP = 32
CY = 64
CX = 512
SWEEPS = 3
TILES = 256
NY = 256
NX = 4096
N_LAT = 4
N_LON = 8


def draw_predicted_quantities(key, part):
    row_pos = jnp.arange(NY, dtype=jnp.float32) / (NY - 1)
    col_pos = jnp.arange(NX, dtype=jnp.float32) / (NX - 1)
    amplitude = 0.1 * jnp.power(10.0, row_pos)[:, None] * jnp.power(10.0, col_pos)[None, :]
    values = jnp.clip(jax.random.normal(key, (3, FIELDS, NY, NX), jnp.float32), -6.0, 6.0)
    return (values * amplitude[None, None]).astype(jnp.bfloat16)


def draw_departing_occupancy(key, part):
    first_key = jax.random.fold_in(key, 11)
    second_key = jax.random.fold_in(key, 12)
    offset = jax.random.randint(first_key, (N_LAT, 1, 1), 0, 4)
    destination = jnp.arange(N_LON, dtype=jnp.int32)[None, None, :]
    busy_dest = (destination + offset) % 4 == 0
    drawn = jax.random.randint(second_key, (N_LAT, N_LON, N_LON), 1, CAP // 2 + 1)
    return jnp.where(busy_dest, CAP, drawn).astype(jnp.int32)


def set_ends(entries, key, least, largest):
    longest = entries.shape.index(max(entries.shape))
    spots = []
    for shift in (0, 1):
        where = [jax.random.randint(jax.random.fold_in(key, axis), (), 0, length) for axis, length in enumerate(entries.shape)]
        where[longest] = (where[longest] + shift) % entries.shape[longest]
        spots.append(tuple(where))
    return entries.at[spots[0]].set(least).at[spots[1]].set(largest)


def block_scale(rng, extent, pieces, smallest, high):
    gain = 1.0
    for dim, shards_of in pieces:
        draws = jax.random.uniform(jax.random.fold_in(jax.random.fold_in(rng, 6), dim), (shards_of,), jnp.float32, smallest / len(pieces), high / len(pieces))
        gain = gain * jnp.repeat(jnp.exp(draws), extent[dim] // shards_of).reshape((-1,) + (1,) * (len(extent) - 1 - dim))
    return gain


def noise(stream_key, dims, width, limit, cuts=(), kind=jnp.bfloat16):
    level = block_scale(stream_key, dims, cuts, -0.22, 0.18) if cuts else 1.0
    array = jax.random.normal(stream_key, dims, jnp.float32) * width * level
    return jnp.minimum(jnp.maximum(array, -limit), limit).astype(kind)


def setup_inputs(seed: int = 0) -> dict:
    splits = jax.random.split(jax.random.key(seed), 7)
    predicted_quantities = draw_predicted_quantities(jax.random.fold_in(splits[6], 71), 0)
    monitor_coefficients = jnp.clip(jnp.exp(jax.random.uniform(splits[1], (FIELDS,), jnp.float32, math.log(0.2), math.log(2.0))), 0.2, 2.0)
    departing_pieces = set_ends(jax.random.randint(splits[2], (N_LAT, N_LON, N_LON, CAP), 0, TILES), jax.random.fold_in(splits[2], 1), 0, TILES - 1).astype(jnp.int32)
    departing_occupancy = draw_departing_occupancy(jax.random.fold_in(splits[6], 71), 0)
    arriving_pieces = set_ends(jax.random.randint(splits[4], (N_LAT, N_LON, N_LON, CAP), 0, TILES), jax.random.fold_in(splits[4], 1), 0, TILES - 1).astype(jnp.int32)
    interpolant_coefficients = noise(splits[5], (N_LAT, N_LON, N_LON, CAP, TILE, TILE), TILE ** -0.5, 0.5, ((0, 4), (1, 8)))
    return {"predicted_quantities": predicted_quantities, "monitor_coefficients": monitor_coefficients, "departing_pieces": departing_pieces, "departing_occupancy": departing_occupancy, "arriving_pieces": arriving_pieces, "interpolant_coefficients": interpolant_coefficients}


def derivatives(potential):
    padded = jnp.pad(potential, ((0, 0), (1, 1)), mode='wrap')
    padded = jnp.pad(padded, ((1, 1), (0, 0)))
    centre = padded[1:-1, 1:-1]
    east = padded[1:-1, 2:]
    west = padded[1:-1, :-2]
    north = padded[2:, 1:-1]
    south = padded[:-2, 1:-1]
    mixed = (padded[2:, 2:] - padded[2:, :-2] - padded[:-2, 2:] + padded[:-2, :-2]) * 0.25
    zonal_derivative = (east - west) * 0.5
    meridional_derivative = (north - south) * 0.5
    second_lon = east - 2.0 * centre + west
    second_lat = north - 2.0 * centre + south
    determinant = (1.0 + second_lon) * (1.0 + second_lat) - mixed * mixed
    return (zonal_derivative, meridional_derivative, determinant)

def spread_values(sent, departing_pieces, departing_occupancy, arriving_pieces, interpolant_coefficients):

    def row_transfer(items):
        lat_index, tile_lists, count_lists, target_lists, weight_row = items
        row_values = lax.dynamic_slice_in_dim(sent, lat_index * CY, CY, 1)
        by_source = row_values.reshape(FIELDS, CY, N_LON, CX // TILE, TILE)
        by_source = by_source.transpose(2, 0, 1, 3, 4).reshape(N_LON, FIELDS, TILES, TILE)
        selected = jax.vmap(lambda source_block, source_ids: jnp.take(source_block, source_ids.reshape(-1), axis=1))(by_source, tile_lists)
        selected = selected.reshape(N_LON, FIELDS, N_LON, CAP, TILE).astype(jnp.float32)
        slot_mask = jnp.arange(CAP, dtype=jnp.int32)[None, None, :] < count_lists[:, :, None]
        selected = jnp.where(slot_mask[:, None, :, :, None], selected, jnp.zeros((), jnp.float32))
        by_dest = selected.transpose(2, 0, 1, 3, 4)

        def dest_sum(inner):
            dest_values, dest_weights, dest_ids = inner
            contrib = jnp.einsum('sfkp,skpq->skfq', dest_values, dest_weights.astype(jnp.float32), precision=lax.Precision.HIGHEST)
            contrib = contrib.reshape(N_LON * CAP, FIELDS, TILE)
            return jax.ops.segment_sum(contrib, dest_ids.reshape(-1), num_segments=TILES)
        summed = lax.map(dest_sum, (by_dest, weight_row, target_lists))
        summed = summed.reshape(N_LON, CY, CX // TILE, FIELDS, TILE)
        return summed.transpose(3, 1, 0, 2, 4).reshape(FIELDS, CY, NX)
    lat_ids = jnp.arange(N_LAT, dtype=jnp.int32)
    result = lax.map(row_transfer, (lat_ids, departing_pieces, departing_occupancy, arriving_pieces, interpolant_coefficients))
    return result.transpose(1, 0, 2, 3).reshape(FIELDS, NY, NX)

def reference(predicted_quantities, monitor_coefficients, departing_pieces, departing_occupancy, arriving_pieces, interpolant_coefficients):
    predicted_states = predicted_quantities.astype(jnp.float32)
    potential = jnp.zeros((NY, NX), jnp.float32)
    scaled = jnp.zeros((NY, NX), jnp.float32)
    for sweep_index in range(SWEEPS):
        zonal_derivative, meridional_derivative, determinant = derivatives(potential)
        displaced_nodes = predicted_states[0] + zonal_derivative[None] * predicted_states[1] + meridional_derivative[None] * predicted_states[2]
        sent = lax.optimization_barrier(displaced_nodes.astype(jnp.bfloat16))
        interp = spread_values(sent, departing_pieces, departing_occupancy, arriving_pieces, interpolant_coefficients)
        blended = displaced_nodes + interp
        monitor = jnp.sqrt(1.0 + lax.optimization_barrier(jnp.sum(monitor_coefficients[:, None, None] * blended * blended, axis=0)))
        balance = monitor * determinant
        target = jnp.mean(balance)
        residual = balance - target
        spread = jnp.sqrt(jnp.mean(residual * residual) + 1e-06)
        potential = potential + 0.5 * residual / (monitor * spread)
        scaled = residual / spread
    return (potential, scaled)
```

```python
import functools

import jax
import jax.numpy as jnp
from jax import lax
from jax.experimental import pallas as pl
from jax.experimental.pallas import tpu as pltpu
from jax.sharding import PartitionSpec as P

FIELDS = 8
TILE = 128
CAP = 32
SWEEPS = 3

VMEM = pltpu.MemorySpace.VMEM
SMEM = pltpu.MemorySpace.SMEM


def pack_tiles(ids_ref, occ_ref, moved_ref, send_ref, rows, blocks):
    def one_dest(d, carry):
        count = occ_ref[d]
        for k in range(CAP):
            tile = ids_ref[d, k]
            row = lax.div(tile, blocks)
            block = lax.rem(tile, blocks)
            values = moved_ref[block, pl.ds(row, FIELDS, stride=rows), :]
            values = jnp.where(k < count, values, jnp.zeros_like(values))
            send_ref[d, k] = values.astype(jnp.bfloat16)
        return carry

    lax.fori_loop(0, ids_ref.shape[0], one_dest, 0)


def first_kernel(ids_ref, occ_ref, pq_ref, moved_ref, send_ref):
    rows, cols = pq_ref.shape[1:]
    blocks = cols // TILE
    for c in range(blocks):
        for f in range(FIELDS):
            moved_ref[c, f * rows : (f + 1) * rows, :] = pq_ref[
                f, :, c * TILE : (c + 1) * TILE
            ].astype(jnp.float32)
    pack_tiles(ids_ref, occ_ref, moved_ref, send_ref, rows, blocks)


def column_to_lanes(column, offset):
    rows = column.shape[0]
    row_id = lax.broadcasted_iota(jnp.int32, (rows, TILE), 0)
    lane_id = lax.broadcasted_iota(jnp.int32, (rows, TILE), 1)
    wide = jnp.broadcast_to(column, (rows, TILE))
    return jnp.sum(jnp.where(lane_id == row_id + offset, wide, 0.0), axis=0, keepdims=True)


def lanes_to_column(lanes, rows, offset):
    row_id = lax.broadcasted_iota(jnp.int32, (rows, TILE), 0)
    lane_id = lax.broadcasted_iota(jnp.int32, (rows, TILE), 1)
    wide = jnp.broadcast_to(lanes, (rows, TILE))
    return jnp.sum(jnp.where(lane_id == row_id + offset, wide, 0.0), axis=1, keepdims=True)


def lane_value(lanes, index):
    lane_id = lax.broadcasted_iota(jnp.int32, lanes.shape, 1)
    return jnp.sum(jnp.where(lane_id == index, lanes, 0.0), axis=1, keepdims=True)


def mesh_place():
    lat, lon = lax.axis_index("lat"), lax.axis_index("lon")
    return lat, lon


def interp_kernel(n_lat, n_lon, has_det, *refs):
    targets_ref, coef_ref, x_ref, w_hbm, moved_ref = refs[:5]
    refs = refs[5:]
    det_ref = None
    if has_det:
        det_ref, refs = refs[0], refs[1:]
    monitor_ref, balance_ref, pay_ref, w_ref, acc_ref, sems = refs
    rows, cols = monitor_ref.shape
    blocks = cols // TILE

    def fetch(s):
        return pltpu.make_async_copy(w_hbm.at[s], w_ref.at[s], sems.at[s])

    for s in range(n_lon):
        fetch(s).start()
    acc_ref[...] = jnp.zeros_like(acc_ref)

    def one_source(s, carry):
        fetch(s).wait()
        for k in range(CAP):
            out = jnp.dot(x_ref[s, k], w_ref[s, k], preferred_element_type=jnp.float32)
            place = pl.ds(pl.multiple_of(targets_ref[s, k] * FIELDS, FIELDS), FIELDS)
            acc_ref[place, :] += out
        return carry

    lax.fori_loop(0, n_lon, one_source, 0)

    for c in range(blocks):
        for b in range(rows // 8):
            total = jnp.ones((8, TILE), jnp.float32)
            for f in range(FIELDS):
                start = (b * 8 * blocks + c) * FIELDS + f
                interp = acc_ref[pl.ds(start, 8, stride=blocks * FIELDS), :]
                blended = moved_ref[c, f * rows + b * 8 : f * rows + b * 8 + 8, :] + interp
                total = total + coef_ref[f] * (blended * blended)
            monitor_ref[b * 8 : b * 8 + 8, c * TILE : (c + 1) * TILE] = jnp.sqrt(total)

    monitor = monitor_ref[...]
    if has_det:
        det = det_ref[...]
        balance = monitor * det
    else:
        det = jnp.ones((rows, cols), jnp.float32)
        balance = monitor
    balance_ref[...] = balance
    inverse = 1.0 / monitor
    count = rows * cols
    mean = jnp.sum(jnp.sum(balance, axis=0, keepdims=True), axis=1, keepdims=True) / count
    away = balance - mean
    squares = jnp.sum(jnp.sum(away * away, axis=0, keepdims=True), axis=1, keepdims=True)
    lane_id = lax.broadcasted_iota(jnp.int32, (1, TILE), 1)
    stats = jnp.where(lane_id == 0, mean, jnp.where(lane_id == 1, squares, 0.0))
    for j in range(n_lat * n_lon):
        pay_ref[j, :, 2 * cols : 2 * cols + TILE] = stats

    lat, lon = mesh_place()
    left = lax.rem(lon + n_lon - 1, n_lon)
    right = lax.rem(lon + 1, n_lon)
    for side, col in ((left, 0), (right, cols - 1)):
        lanes = column_to_lanes(det[:, col : col + 1], 0)
        lanes = lanes + column_to_lanes(inverse[:, col : col + 1], rows)
        pay_ref[lat * n_lon + side, :, 0:TILE] = lanes

    def send_row(other, row):
        pay_ref[other * n_lon + lon, :, 0:cols] = det[row : row + 1, :]
        pay_ref[other * n_lon + lon, :, cols : 2 * cols] = inverse[row : row + 1, :]
        for side, col in ((left, 0), (right, cols - 1)):
            lanes = jnp.where(
                lane_id == 0,
                det[row : row + 1, col : col + 1],
                inverse[row : row + 1, col : col + 1],
            )
            pay_ref[other * n_lon + side, :, 0:TILE] = lanes

    @pl.when(lat > 0)
    def _():
        send_row(lat - 1, 0)

    @pl.when(lat < n_lat - 1)
    def _():
        send_row(lat + 1, rows - 1)


def whole_stats(got_ref, n_dev, count, stat_at):
    total = got_ref[0, :, stat_at : stat_at + TILE]
    for j in range(1, n_dev):
        total = total + got_ref[j, :, stat_at : stat_at + TILE]
    target = lane_value(total, 0) / n_dev
    apart = jnp.zeros((1, TILE), jnp.float32)
    for j in range(n_dev):
        away = got_ref[j, :, stat_at : stat_at + TILE] - target
        apart = apart + away * away
    variance = (lane_value(total, 1) / count + lane_value(apart, 0)) / n_dev
    return target, jnp.sqrt(variance + 1e-06)


def update_kernel(n_lat, n_lon, n_got, *refs):
    ids_ref, occ_ref = refs[:2]
    got_refs = refs[2 : 2 + n_got]
    refs = refs[2 + n_got :]
    if n_got > 1:
        old_ref, refs = refs[0], refs[1:]
    monitor_ref, balance_ref, pq_ref, pot_ref, det_ref, moved_ref, send_ref = refs
    rows, cols = monitor_ref.shape
    blocks = cols // TILE
    n_dev = n_lat * n_lon
    lat, lon = mesh_place()
    left = lax.rem(lon + n_lon - 1, n_lon)
    right = lax.rem(lon + 1, n_lon)
    below = jnp.maximum(lat - 1, 0)
    above = jnp.minimum(lat + 1, n_lat - 1)

    south_row = jnp.zeros((1, cols), jnp.float32)
    north_row = jnp.zeros((1, cols), jnp.float32)
    sides = [jnp.zeros((rows, 1), jnp.float32)] * 2
    corners = [jnp.zeros((1, 1), jnp.float32)] * 4
    for got_ref in got_refs:
        target, spread = whole_stats(got_ref, n_dev, rows * cols, 2 * cols)

        def gain(det, inverse):
            return 0.5 * (det - target * inverse) / spread

        def row_from(j):
            return gain(got_ref[j, :, 0:cols], got_ref[j, :, cols : 2 * cols])

        south_row = south_row + row_from(below * n_lon + lon)
        north_row = north_row + row_from(above * n_lon + lon)
        for i, side in enumerate((left, right)):
            lanes = got_ref[lat * n_lon + side, :, 0:TILE]
            sides[i] = sides[i] + gain(
                lanes_to_column(lanes, rows, 0), lanes_to_column(lanes, rows, rows)
            )
        for i, (other, side) in enumerate(
            ((below, left), (below, right), (above, left), (above, right))
        ):
            lanes = got_ref[other * n_lon + side, :, 0:TILE]
            corners[i] = corners[i] + gain(lane_value(lanes, 0), lane_value(lanes, 1))

    has_south, has_north = lat > 0, lat < n_lat - 1
    south_row = jnp.where(has_south, south_row, 0.0)
    north_row = jnp.where(has_north, north_row, 0.0)
    corners = [
        jnp.where(has, corner, 0.0)
        for has, corner in zip((has_south, has_south, has_north, has_north), corners)
    ]

    potential = 0.5 * (balance_ref[...] - target) / (monitor_ref[...] * spread)
    if n_got > 1:
        potential = old_ref[...] + potential
    pot_ref[...] = potential

    row_id = lax.broadcasted_iota(jnp.int32, (rows, cols), 0)
    lane_id = lax.broadcasted_iota(jnp.int32, (rows, cols), 1)
    first, last = row_id == 0, row_id == rows - 1
    west_edge, east_edge = lane_id == 0, lane_id == cols - 1
    north = jnp.where(last, north_row, pltpu.roll(potential, rows - 1, 0))
    south = jnp.where(first, south_row, pltpu.roll(potential, 1, 0))
    east = jnp.where(east_edge, sides[1], pltpu.roll(potential, cols - 1, 1))
    west = jnp.where(west_edge, sides[0], pltpu.roll(potential, 1, 1))
    zonal = (east - west) * 0.5
    tall = north - south
    meridional = tall * 0.5

    for c in range(blocks):
        lanes = slice(c * TILE, (c + 1) * TILE)
        for f in range(FIELDS):
            value = (
                pq_ref[0, f, :, lanes].astype(jnp.float32)
                + zonal[:, lanes] * pq_ref[1, f, :, lanes].astype(jnp.float32)
                + meridional[:, lanes] * pq_ref[2, f, :, lanes].astype(jnp.float32)
            )
            moved_ref[c, f * rows : (f + 1) * rows, :] = value
    pack_tiles(ids_ref, occ_ref, moved_ref, send_ref, rows, blocks)

    small_row = lax.broadcasted_iota(jnp.int32, (rows, TILE), 0)

    def side_tall(column, low, high):
        wide = jnp.broadcast_to(column, (rows, TILE))
        up = jnp.where(small_row == rows - 1, high, pltpu.roll(wide, rows - 1, 0))
        down = jnp.where(small_row == 0, low, pltpu.roll(wide, 1, 0))
        return (up - down)[:, 0:1]

    west_tall = side_tall(sides[0], corners[0], corners[2])
    east_tall = side_tall(sides[1], corners[1], corners[3])
    tall_east = jnp.where(east_edge, east_tall, pltpu.roll(tall, cols - 1, 1))
    tall_west = jnp.where(west_edge, west_tall, pltpu.roll(tall, 1, 1))
    mixed = (tall_east - tall_west) * 0.25
    second_lon = east - 2.0 * potential + west
    second_lat = north - 2.0 * potential + south
    det_ref[...] = (1.0 + second_lon) * (1.0 + second_lat) - mixed * mixed


def last_kernel(n_dev, got_ref, old_ref, monitor_ref, balance_ref, pot_ref, scaled_ref):
    rows, cols = monitor_ref.shape
    target, spread = whole_stats(got_ref, n_dev, rows * cols, 0)
    residual = balance_ref[...] - target
    scaled_ref[...] = residual / spread
    pot_ref[...] = old_ref[...] + 0.5 * residual / (monitor_ref[...] * spread)


def per_device(pq, coef, departing, occupancy, arriving, blocks_w):
    n_lat, n_lon = lax.axis_size("lat"), lax.axis_size("lon")
    n_dev = n_lat * n_lon
    rows, cols = pq.shape[2:]
    ids = departing[0, 0]
    occ = occupancy[0, 0]
    targets = arriving[0, 0]
    weights = blocks_w[0, 0]
    smem = pl.BlockSpec(memory_space=SMEM)
    vmem = pl.BlockSpec(memory_space=VMEM)
    hbm = pl.BlockSpec(memory_space=pl.ANY)
    f32 = jnp.float32
    grid = jax.ShapeDtypeStruct((rows, cols), f32)
    moved_shape = jax.ShapeDtypeStruct((cols // TILE, FIELDS * rows, TILE), f32)
    send_shape = jax.ShapeDtypeStruct((n_lon, CAP, FIELDS, TILE), jnp.bfloat16)
    pay_shape = jax.ShapeDtypeStruct((n_dev, 1, 2 * cols + TILE), f32)
    params = pltpu.CompilerParams(vmem_limit_bytes=48 << 20)

    moved, send = pl.pallas_call(
        first_kernel,
        out_shape=(moved_shape, send_shape),
        grid=(1,),
        in_specs=[
            smem,
            smem,
            pl.BlockSpec((pl.Squeezed(), FIELDS, rows, cols), lambda i: (0, 0, 0, 0)),
        ],
        out_specs=(
            pl.BlockSpec(moved_shape.shape, lambda i: (0, 0, 0)),
            pl.BlockSpec(send_shape.shape, lambda i: (0, 0, 0, 0)),
        ),
        compiler_params=params,
        name="first",
    )(ids, occ, pq)

    def interp(send, moved, det):
        got = lax.all_to_all(send, "lon", 0, 0, tiled=True)
        args = [targets, coef, got, weights, moved]
        specs = [smem, smem, vmem, hbm, vmem]
        if det is not None:
            args.append(det)
            specs.append(vmem)
        return pl.pallas_call(
            functools.partial(interp_kernel, n_lat, n_lon, det is not None),
            out_shape=(grid, grid, pay_shape),
            in_specs=specs,
            out_specs=(vmem, vmem, vmem),
            scratch_shapes=[
                pltpu.VMEM((n_lon, CAP, TILE, TILE), jnp.bfloat16),
                pltpu.VMEM((FIELDS * rows * cols // TILE, TILE), f32),
                pltpu.SemaphoreType.DMA((n_lon,)),
            ],
            compiler_params=params,
            name="interp",
        )(*args)

    def share(pay):
        return lax.all_to_all(pay, ("lat", "lon"), 0, 0, tiled=True)

    gots = []
    potential = det = None
    for sweep in range(SWEEPS):
        monitor, balance, pay = interp(send, moved, det)
        if sweep == SWEEPS - 1:
            break
        gots.append(share(pay))
        olds = [] if potential is None else [potential]
        potential, det, moved, send = pl.pallas_call(
            functools.partial(update_kernel, n_lat, n_lon, len(gots)),
            out_shape=(grid, grid, moved_shape, send_shape),
            in_specs=[smem, smem] + [vmem] * (len(gots) + len(olds) + 3),
            out_specs=(vmem,) * 4,
            compiler_params=params,
            name="update",
        )(ids, occ, *gots, *olds, monitor, balance, pq)

    got = share(pay[:, :, 2 * cols :])
    return pl.pallas_call(
        functools.partial(last_kernel, n_dev),
        out_shape=(grid, grid),
        in_specs=[vmem] * 4,
        out_specs=(vmem, vmem),
        compiler_params=params,
        name="last",
    )(got, potential, monitor, balance)


def solution(mesh):
    in_specs = (
        P(None, None, "lat", "lon"),
        P(),
        P("lat", "lon", None, None),
        P("lat", "lon", None),
        P("lat", "lon", None, None),
        P("lat", "lon", None, None, None, None),
    )
    out_specs = (P("lat", "lon"), P("lat", "lon"))
    return jax.shard_map(
        per_device, mesh=mesh, in_specs=in_specs, out_specs=out_specs, check_vma=False
    )
```

```python
import functools

import jax
import jax.numpy as jnp
from jax import lax
from jax.experimental import pallas as pl
from jax.experimental.pallas import tpu as pltpu
from jax.sharding import PartitionSpec as P

FIELDS = 8
TILE = 128
CAP = 32
SWEEPS = 3

VMEM = pltpu.MemorySpace.VMEM
SMEM = pltpu.MemorySpace.SMEM


def to_tiles(pq_ref, out_ref):
    fields, rows, cols = pq_ref.shape
    blocks = cols // TILE
    for b in range(rows // 16):
        for c in range(blocks):
            part = pq_ref[:, b * 16 : b * 16 + 16, c * TILE : (c + 1) * TILE]
            part = jnp.transpose(part.astype(jnp.float32), (1, 0, 2))
            for i in range(16):
                start = ((b * 16 + i) * blocks + c) * fields
                out_ref[start : start + fields, :] = part[i]


def pack_tiles(ids_ref, occ_ref, moved_ref, send_ref):
    def one_dest(d, carry):
        count = occ_ref[d]
        for k in range(0, CAP, 2):
            pair = []
            for i in (k, k + 1):
                start = pl.multiple_of(ids_ref[d, i] * FIELDS, FIELDS)
                values = moved_ref[pl.ds(start, FIELDS), :]
                pair.append(jnp.where(i < count, values, jnp.zeros_like(values)))
            place = pl.multiple_of((d * CAP + k) * FIELDS, 2 * FIELDS)
            send_ref[pl.ds(place, 2 * FIELDS), :] = jnp.concatenate(pair, axis=0).astype(
                jnp.bfloat16
            )
        return carry

    lax.fori_loop(0, ids_ref.shape[0], one_dest, 0)


def first_kernel(early, *refs):
    ids_hbm, occ_hbm, targets_hbm, coef_hbm, pq_hbm, w_hbm = refs[:6]
    send_ref, still_ref, lon_ref, lat_ref, targets_ref, coef_ref, w_ref = refs[6:13]
    ids_ref, occ_ref, pq_ref, sems = refs[13:]
    fields = [
        pltpu.make_async_copy(pq_hbm.at[i], pq_ref.at[i], sems.at[i]) for i in range(3)
    ]
    lists = [
        pltpu.make_async_copy(ids_hbm, ids_ref, sems.at[3]),
        pltpu.make_async_copy(occ_hbm, occ_ref, sems.at[4]),
    ]
    later = [
        pltpu.make_async_copy(targets_hbm, targets_ref, sems.at[5]),
        pltpu.make_async_copy(coef_hbm, coef_ref, sems.at[6]),
        pltpu.make_async_copy(w_hbm.at[pl.ds(0, early)], w_ref, sems.at[7]),
    ]
    for copy in (fields[0], *lists, *fields[1:], *later):
        copy.start()
    fields[0].wait()
    to_tiles(pq_ref.at[0], still_ref)
    for copy in lists:
        copy.wait()
    pack_tiles(ids_ref, occ_ref, still_ref, send_ref)
    for i, out_ref in ((1, lon_ref), (2, lat_ref)):
        fields[i].wait()
        to_tiles(pq_ref.at[i], out_ref)
    for copy in later:
        copy.wait()


def sum_fields(tiles):
    sub = lax.broadcasted_iota(jnp.int32, (8, TILE), 0)
    high = (sub & 4) == 0
    pairs = []
    for i in range(4):
        one, two = tiles[i], tiles[i + 4]
        kept, moving = jnp.where(high, one, two), jnp.where(high, two, one)
        pairs.append(kept + pltpu.roll(moving, 4, 0))
    for step in (2, 1):
        near = (sub & step) == 0
        pairs = [
            jnp.where(
                near,
                pairs[i] + pltpu.roll(pairs[i], 8 - step, 0),
                pairs[i + step] + pltpu.roll(pairs[i + step], step, 0),
            )
            for i in range(step)
        ]
    return pairs[0]


def column_to_lanes(column, offset):
    rows = column.shape[0]
    row_id = lax.broadcasted_iota(jnp.int32, (rows, TILE), 0)
    lane_id = lax.broadcasted_iota(jnp.int32, (rows, TILE), 1)
    wide = jnp.broadcast_to(column, (rows, TILE))
    return jnp.sum(jnp.where(lane_id == row_id + offset, wide, 0.0), axis=0, keepdims=True)


def lanes_to_column(lanes, rows, offset):
    row_id = lax.broadcasted_iota(jnp.int32, (rows, TILE), 0)
    lane_id = lax.broadcasted_iota(jnp.int32, (rows, TILE), 1)
    wide = jnp.broadcast_to(lanes, (rows, TILE))
    return jnp.sum(jnp.where(lane_id == row_id + offset, wide, 0.0), axis=1, keepdims=True)


def lane_value(lanes, index):
    lane_id = lax.broadcasted_iota(jnp.int32, lanes.shape, 1)
    return jnp.sum(jnp.where(lane_id == index, lanes, 0.0), axis=1, keepdims=True)


def mesh_place():
    lat, lon = lax.axis_index("lat"), lax.axis_index("lon")
    return lat, lon


def interp_kernel(n_lat, n_lon, early, start_sweep, *refs):
    targets_ref, coef_ref, x_ref, early_ref, late_hbm, moved_ref = refs[:6]
    if start_sweep:
        monitor_ref, balance_ref, pay_ref, late_ref, acc_ref, sems = refs[6:]
    else:
        late_ref = late_hbm
        det_ref, monitor_ref, balance_ref, pay_ref, acc_ref = refs[6:]
    rows, cols = monitor_ref.shape
    blocks = cols // TILE

    def fetch(s):
        return pltpu.make_async_copy(late_hbm.at[early + s], late_ref.at[s], sems.at[s])

    if start_sweep:
        for s in range(n_lon - early):
            fetch(s).start()
    acc_ref[...] = jnp.zeros_like(acc_ref)

    def add_source(s, w_ref, first_source):
        for k in range(0, CAP, 2):
            slot = pl.multiple_of(((s + first_source) * CAP + k) * FIELDS, 2 * FIELDS)
            pair = jnp.concatenate([w_ref[s, k], w_ref[s, k + 1]], axis=1)
            out = jnp.dot(
                x_ref[pl.ds(slot, 2 * FIELDS), :], pair, preferred_element_type=jnp.float32
            )
            for i in (0, 1):
                target = targets_ref[s + first_source, k + i]
                place = pl.ds(pl.multiple_of(target * FIELDS, FIELDS), FIELDS)
                acc_ref[place, :] += out[
                    i * FIELDS : (i + 1) * FIELDS, i * TILE : (i + 1) * TILE
                ]

    def one_early(s, carry):
        add_source(s, early_ref, 0)
        return carry

    def one_late(s, carry):
        if start_sweep:
            fetch(s).wait()
        add_source(s, late_ref, early)
        return carry

    lax.fori_loop(0, early, one_early, 0)
    lax.fori_loop(0, n_lon - early, one_late, 0)

    field_id = lax.broadcasted_iota(jnp.int32, (FIELDS, TILE), 0)
    coef = jnp.zeros((FIELDS, TILE), jnp.float32)
    for f in range(FIELDS):
        coef = jnp.where(field_id == f, coef_ref[f], coef)
    for b in range(rows // 8):
        for c in range(blocks):
            parts = []
            for i in range(8):
                start = ((b * 8 + i) * blocks + c) * FIELDS
                place = slice(start, start + FIELDS)
                blended = moved_ref[place, :] + acc_ref[place, :]
                parts.append(coef * (blended * blended))
            monitor_ref[b * 8 : b * 8 + 8, c * TILE : (c + 1) * TILE] = jnp.sqrt(
                1.0 + sum_fields(parts)
            )

    monitor = monitor_ref[...]
    if start_sweep:
        det = jnp.ones((rows, cols), jnp.float32)
        balance = monitor
    else:
        det = det_ref[...]
        balance = monitor * det
    balance_ref[...] = balance
    inverse = 1.0 / monitor
    count = rows * cols
    mean = jnp.sum(jnp.sum(balance, axis=0, keepdims=True), axis=1, keepdims=True) / count
    away = balance - mean
    squares = jnp.sum(jnp.sum(away * away, axis=0, keepdims=True), axis=1, keepdims=True)
    lane_id = lax.broadcasted_iota(jnp.int32, (1, TILE), 1)
    stats = jnp.where(lane_id == 0, mean, jnp.where(lane_id == 1, squares, 0.0))
    for j in range(n_lat * n_lon):
        pay_ref[j, :, 2 * cols : 2 * cols + TILE] = stats

    lat, lon = mesh_place()
    left = lax.rem(lon + n_lon - 1, n_lon)
    right = lax.rem(lon + 1, n_lon)
    for side, col in ((left, 0), (right, cols - 1)):
        lanes = column_to_lanes(det[:, col : col + 1], 0)
        lanes = lanes + column_to_lanes(inverse[:, col : col + 1], rows)
        pay_ref[lat * n_lon + side, :, 0:TILE] = lanes

    def send_row(other, row):
        pay_ref[other * n_lon + lon, :, 0:cols] = det[row : row + 1, :]
        pay_ref[other * n_lon + lon, :, cols : 2 * cols] = inverse[row : row + 1, :]
        for side, col in ((left, 0), (right, cols - 1)):
            lanes = jnp.where(
                lane_id == 0,
                det[row : row + 1, col : col + 1],
                inverse[row : row + 1, col : col + 1],
            )
            pay_ref[other * n_lon + side, :, 0:TILE] = lanes

    @pl.when(lat > 0)
    def _():
        send_row(lat - 1, 0)

    @pl.when(lat < n_lat - 1)
    def _():
        send_row(lat + 1, rows - 1)


def whole_stats(got_ref, n_dev, count, stat_at):
    total = got_ref[0, :, stat_at : stat_at + TILE]
    for j in range(1, n_dev):
        total = total + got_ref[j, :, stat_at : stat_at + TILE]
    target = lane_value(total, 0) / n_dev
    apart = jnp.zeros((1, TILE), jnp.float32)
    for j in range(n_dev):
        away = got_ref[j, :, stat_at : stat_at + TILE] - target
        apart = apart + away * away
    variance = (lane_value(total, 1) / count + lane_value(apart, 0)) / n_dev
    return target, jnp.sqrt(variance + 1e-06)


def update_kernel(n_lat, n_lon, n_got, *refs):
    ids_ref, occ_ref = refs[:2]
    got_refs = refs[2 : 2 + n_got]
    refs = refs[2 + n_got :]
    if n_got > 1:
        old_ref, refs = refs[0], refs[1:]
    (
        monitor_ref,
        balance_ref,
        still_ref,
        lon_ref,
        lat_ref,
        pot_ref,
        det_ref,
        moved_ref,
        send_ref,
        zonal_ref,
        meridional_ref,
    ) = refs
    rows, cols = monitor_ref.shape
    blocks = cols // TILE
    n_dev = n_lat * n_lon
    lat, lon = mesh_place()
    left = lax.rem(lon + n_lon - 1, n_lon)
    right = lax.rem(lon + 1, n_lon)
    below = jnp.maximum(lat - 1, 0)
    above = jnp.minimum(lat + 1, n_lat - 1)

    south_row = jnp.zeros((1, cols), jnp.float32)
    north_row = jnp.zeros((1, cols), jnp.float32)
    sides = [jnp.zeros((rows, 1), jnp.float32)] * 2
    corners = [jnp.zeros((1, 1), jnp.float32)] * 4
    for got_ref in got_refs:
        target, spread = whole_stats(got_ref, n_dev, rows * cols, 2 * cols)

        def gain(det, inverse):
            return 0.5 * (det - target * inverse) / spread

        def row_from(j):
            return gain(got_ref[j, :, 0:cols], got_ref[j, :, cols : 2 * cols])

        south_row = south_row + row_from(below * n_lon + lon)
        north_row = north_row + row_from(above * n_lon + lon)
        for i, side in enumerate((left, right)):
            lanes = got_ref[lat * n_lon + side, :, 0:TILE]
            sides[i] = sides[i] + gain(
                lanes_to_column(lanes, rows, 0), lanes_to_column(lanes, rows, rows)
            )
        for i, (other, side) in enumerate(
            ((below, left), (below, right), (above, left), (above, right))
        ):
            lanes = got_ref[other * n_lon + side, :, 0:TILE]
            corners[i] = corners[i] + gain(lane_value(lanes, 0), lane_value(lanes, 1))

    has_south, has_north = lat > 0, lat < n_lat - 1
    south_row = jnp.where(has_south, south_row, 0.0)
    north_row = jnp.where(has_north, north_row, 0.0)
    corners = [
        jnp.where(has, corner, 0.0)
        for has, corner in zip((has_south, has_south, has_north, has_north), corners)
    ]

    potential = 0.5 * (balance_ref[...] - target) / (monitor_ref[...] * spread)
    if n_got > 1:
        potential = old_ref[...] + potential
    pot_ref[...] = potential

    row_id = lax.broadcasted_iota(jnp.int32, (rows, cols), 0)
    lane_id = lax.broadcasted_iota(jnp.int32, (rows, cols), 1)
    first, last = row_id == 0, row_id == rows - 1
    west_edge, east_edge = lane_id == 0, lane_id == cols - 1
    north = jnp.where(last, north_row, pltpu.roll(potential, rows - 1, 0))
    south = jnp.where(first, south_row, pltpu.roll(potential, 1, 0))
    east = jnp.where(east_edge, sides[1], pltpu.roll(potential, cols - 1, 1))
    west = jnp.where(west_edge, sides[0], pltpu.roll(potential, 1, 1))
    tall = north - south
    zonal_ref[...] = (east - west) * 0.5
    meridional_ref[...] = tall * 0.5

    for r in range(rows):
        for c in range(blocks):
            lanes = slice(c * TILE, (c + 1) * TILE)
            start = (r * blocks + c) * FIELDS
            place = slice(start, start + FIELDS)
            zonal = jnp.broadcast_to(zonal_ref[r : r + 1, lanes], (FIELDS, TILE))
            meridional = jnp.broadcast_to(meridional_ref[r : r + 1, lanes], (FIELDS, TILE))
            moved_ref[place, :] = (
                still_ref[place, :]
                + zonal * lon_ref[place, :]
                + meridional * lat_ref[place, :]
            )
    pack_tiles(ids_ref, occ_ref, moved_ref, send_ref)

    small_row = lax.broadcasted_iota(jnp.int32, (rows, TILE), 0)

    def side_tall(column, low, high):
        wide = jnp.broadcast_to(column, (rows, TILE))
        up = jnp.where(small_row == rows - 1, high, pltpu.roll(wide, rows - 1, 0))
        down = jnp.where(small_row == 0, low, pltpu.roll(wide, 1, 0))
        return (up - down)[:, 0:1]

    west_tall = side_tall(sides[0], corners[0], corners[2])
    east_tall = side_tall(sides[1], corners[1], corners[3])
    tall_east = jnp.where(east_edge, east_tall, pltpu.roll(tall, cols - 1, 1))
    tall_west = jnp.where(west_edge, west_tall, pltpu.roll(tall, 1, 1))
    mixed = (tall_east - tall_west) * 0.25
    second_lon = east - 2.0 * potential + west
    second_lat = north - 2.0 * potential + south
    det_ref[...] = (1.0 + second_lon) * (1.0 + second_lat) - mixed * mixed


def last_kernel(n_dev, got_ref, old_ref, monitor_ref, balance_ref, pot_ref, scaled_ref):
    rows, cols = monitor_ref.shape
    target, spread = whole_stats(got_ref, n_dev, rows * cols, 0)
    residual = balance_ref[...] - target
    scaled_ref[...] = residual / spread
    pot_ref[...] = old_ref[...] + 0.5 * residual / (monitor_ref[...] * spread)


def per_device(pq, coef, departing, occupancy, arriving, blocks_w):
    n_lat, n_lon = lax.axis_size("lat"), lax.axis_size("lon")
    n_dev = n_lat * n_lon
    rows, cols = pq.shape[2:]
    ids = departing[0, 0]
    occ = occupancy[0, 0]
    targets = arriving[0, 0]
    weights = blocks_w[0, 0]
    smem = pl.BlockSpec(memory_space=SMEM)
    vmem = pl.BlockSpec(memory_space=VMEM)
    hbm = pl.BlockSpec(memory_space=pltpu.MemorySpace.HBM)
    f32 = jnp.float32
    grid = jax.ShapeDtypeStruct((rows, cols), f32)
    tile_rows = FIELDS * rows * cols // TILE
    moved_shape = jax.ShapeDtypeStruct((tile_rows, TILE), f32)
    send_shape = jax.ShapeDtypeStruct((n_lon * CAP * FIELDS, TILE), jnp.bfloat16)
    pay_shape = jax.ShapeDtypeStruct((n_dev, 1, 2 * cols + TILE), f32)
    params = pltpu.CompilerParams(vmem_limit_bytes=5 << 20)

    def in_hbm(array):
        return pltpu.with_memory_space_constraint(array, pltpu.MemorySpace.HBM)

    def in_vmem(shape):
        return VMEM(shape.shape, shape.dtype)

    early = n_lon // 2
    block = (CAP, TILE, TILE)
    early_shape = jax.ShapeDtypeStruct((early,) + block, weights.dtype)
    late_shape = jax.ShapeDtypeStruct((n_lon - early,) + block, weights.dtype)
    send, still, lon_part, lat_part, targets, coef, w_early = pl.pallas_call(
        functools.partial(first_kernel, early),
        out_shape=(send_shape,)
        + (moved_shape,) * 3
        + (
            jax.ShapeDtypeStruct(targets.shape, targets.dtype),
            jax.ShapeDtypeStruct(coef.shape, coef.dtype),
            in_vmem(early_shape),
        ),
        in_specs=[hbm] * 6,
        out_specs=(vmem,) * 7,
        scratch_shapes=[
            pltpu.SMEM(ids.shape, jnp.int32),
            pltpu.SMEM(occ.shape, jnp.int32),
            pltpu.VMEM(pq.shape, pq.dtype),
            pltpu.SemaphoreType.DMA((8,)),
        ],
        compiler_params=params,
        name="first",
    )(*[in_hbm(x) for x in (ids, occ, targets, coef, pq, weights)])
    tiles = (still, lon_part, lat_part)
    moved = still
    w_late = None

    def interp(send, moved, det, w_late):
        got = lax.all_to_all(send.reshape(n_lon, -1, TILE), "lon", 0, 0, tiled=True)
        start_sweep = det is None
        args = [targets, coef, got.reshape(send.shape), w_early]
        out_shape = [grid, grid, pay_shape]
        scratch = [pltpu.VMEM((tile_rows, TILE), f32)]
        if start_sweep:
            args += [in_hbm(weights), moved]
            out_shape.append(in_vmem(late_shape))
            scratch.append(pltpu.SemaphoreType.DMA((n_lon - early,)))
        else:
            args += [w_late, moved, det]
        return pl.pallas_call(
            functools.partial(interp_kernel, n_lat, n_lon, early, start_sweep),
            out_shape=tuple(out_shape),
            in_specs=[smem, smem, vmem, vmem, hbm if start_sweep else vmem]
            + [vmem] * (len(args) - 5),
            out_specs=(vmem,) * len(out_shape),
            scratch_shapes=scratch,
            compiler_params=params,
            name="interp",
        )(*args)

    def share(pay):
        return lax.all_to_all(pay, ("lat", "lon"), 0, 0, tiled=True)

    gots = []
    potential = det = None
    for sweep in range(SWEEPS):
        monitor, balance, pay, *late = interp(send, moved, det, w_late)
        w_late = late[0] if late else w_late
        if sweep == SWEEPS - 1:
            break
        gots.append(share(pay))
        olds = [] if potential is None else [potential]
        potential, det, moved, send = pl.pallas_call(
            functools.partial(update_kernel, n_lat, n_lon, len(gots)),
            out_shape=(grid, grid, moved_shape, send_shape),
            in_specs=[smem, smem] + [vmem] * (len(gots) + len(olds) + 5),
            out_specs=(vmem,) * 4,
            scratch_shapes=[pltpu.VMEM((rows, cols), f32)] * 2,
            compiler_params=params,
            name="update",
        )(ids, occ, *gots, *olds, monitor, balance, *tiles)

    got = share(pay[:, :, 2 * cols :])
    return pl.pallas_call(
        functools.partial(last_kernel, n_dev),
        out_shape=(grid, grid),
        in_specs=[vmem] * 4,
        out_specs=(vmem, vmem),
        compiler_params=params,
        name="last",
    )(got, potential, monitor, balance)


def solution(mesh):
    in_specs = (
        P(None, None, "lat", "lon"),
        P(),
        P("lat", "lon", None, None),
        P("lat", "lon", None),
        P("lat", "lon", None, None),
        P("lat", "lon", None, None, None, None),
    )
    out_specs = (P("lat", "lon"), P("lat", "lon"))
    return jax.shard_map(
        per_device, mesh=mesh, in_specs=in_specs, out_specs=out_specs, check_vma=False
    )
```

```python
import functools

import jax
import jax.numpy as jnp
from jax import lax
from jax.experimental import pallas as pl
from jax.experimental.pallas import tpu as pltpu
from jax.sharding import PartitionSpec as P

FIELDS = 8
TILE = 128
CAP = 32
SWEEPS = 3


VMEM = pltpu.MemorySpace.VMEM
SMEM = pltpu.MemorySpace.SMEM


def to_tiles(pq_ref, out_ref):
    fields, rows, cols = pq_ref.shape
    blocks = cols // TILE
    for b in range(rows // 16):
        for c in range(blocks):
            part = pq_ref[:, b * 16 : b * 16 + 16, c * TILE : (c + 1) * TILE]
            part = jnp.transpose(part.astype(jnp.float32), (1, 0, 2))
            for i in range(16):
                start = ((b * 16 + i) * blocks + c) * fields
                out_ref[start : start + fields, :] = part[i]


def pack_tiles(lon, rows_ref, moved_ref, send_refs):
    for r, send_ref in enumerate(send_refs):
        dest = lon ^ r
        for k in range(0, CAP, 2):
            pair = []
            for i in (k, k + 1):
                start = pl.multiple_of(rows_ref[dest, i], FIELDS)
                pair.append(moved_ref[pl.ds(start, FIELDS), :])
            send_ref[k * FIELDS : (k + 2) * FIELDS, :] = jnp.concatenate(pair, axis=0).astype(
                jnp.bfloat16
            )


def zero_tile(moved_ref):
    moved_ref[moved_ref.shape[0] - FIELDS :, :] = jnp.zeros((FIELDS, TILE), jnp.float32)


def first_kernel(n_lon, *refs):
    ids_hbm, occ_hbm, targets_hbm, coef_hbm, pq_hbm = refs[:5]
    still_ref, rows_ref, targets_ref, coef_ref = refs[5:9]
    send_refs, (ids_ref, occ_ref, place_ref, pq_ref, sems) = refs[9:-5], refs[-5:]
    fields = pltpu.make_async_copy(pq_hbm.at[0], pq_ref, sems.at[0])
    lists = [
        pltpu.make_async_copy(ids_hbm, ids_ref, sems.at[1]),
        pltpu.make_async_copy(occ_hbm, occ_ref, sems.at[2]),
    ]
    later = [
        pltpu.make_async_copy(targets_hbm, targets_ref, sems.at[3]),
        pltpu.make_async_copy(coef_hbm, coef_ref, sems.at[4]),
    ]
    for copy in (*lists, fields, *later):
        copy.start()
    zero_tile(still_ref)
    for copy in lists:
        copy.wait()
    dest_id = lax.broadcasted_iota(jnp.int32, (n_lon, CAP), 0)
    slot_id = lax.broadcasted_iota(jnp.int32, (n_lon, CAP), 1)
    count = jnp.zeros((n_lon, CAP), jnp.int32)
    for d in range(n_lon):
        count = jnp.where(dest_id == d, occ_ref[d], count)
    zero_row = still_ref.shape[0] - FIELDS
    rows_ref[...] = jnp.where(slot_id < count, ids_ref[...] * FIELDS, zero_row)
    places = pltpu.make_async_copy(rows_ref, place_ref, sems.at[1])
    places.start()
    fields.wait()
    to_tiles(pq_ref, still_ref)
    places.wait()
    pack_tiles(lax.axis_index("lon"), place_ref, still_ref, send_refs)
    for copy in later:
        copy.wait()


def sum_fields(tiles):
    sub = lax.broadcasted_iota(jnp.int32, (8, TILE), 0)
    high = (sub & 4) == 0
    pairs = []
    for i in range(4):
        one, two = tiles[i], tiles[i + 4]
        kept, moving = jnp.where(high, one, two), jnp.where(high, two, one)
        pairs.append(kept + pltpu.roll(moving, 4, 0))
    for step in (2, 1):
        near = (sub & step) == 0
        pairs = [
            jnp.where(
                near,
                pairs[i] + pltpu.roll(pairs[i], 8 - step, 0),
                pairs[i + step] + pltpu.roll(pairs[i + step], step, 0),
            )
            for i in range(step)
        ]
    return pairs[0]


def column_to_lanes(column, offset):
    rows = column.shape[0]
    row_id = lax.broadcasted_iota(jnp.int32, (rows, TILE), 0)
    lane_id = lax.broadcasted_iota(jnp.int32, (rows, TILE), 1)
    wide = jnp.broadcast_to(column, (rows, TILE))
    return jnp.sum(jnp.where(lane_id == row_id + offset, wide, 0.0), axis=0, keepdims=True)


def lanes_to_column(lanes, rows, offset):
    row_id = lax.broadcasted_iota(jnp.int32, (rows, TILE), 0)
    lane_id = lax.broadcasted_iota(jnp.int32, (rows, TILE), 1)
    wide = jnp.broadcast_to(lanes, (rows, TILE))
    return jnp.sum(jnp.where(lane_id == row_id + offset, wide, 0.0), axis=1, keepdims=True)


def lane_value(lanes, index):
    lane_id = lax.broadcasted_iota(jnp.int32, lanes.shape, 1)
    return jnp.sum(jnp.where(lane_id == index, lanes, 0.0), axis=1, keepdims=True)


def mesh_place():
    lat, lon = lax.axis_index("lat"), lax.axis_index("lon")
    return lat, lon


def add_source(source, local, targets_ref, x_ref, w_ref, acc_ref):
    for k in range(0, CAP, 2):
        pair = jnp.concatenate([w_ref[local, k], w_ref[local, k + 1]], axis=1)
        out = jnp.dot(
            x_ref[k * FIELDS : (k + 2) * FIELDS, :], pair, preferred_element_type=jnp.float32
        )
        for i in (0, 1):
            start = pl.multiple_of(targets_ref[source, k + i] * FIELDS, FIELDS)
            acc_ref[pl.ds(start, FIELDS), :] += out[
                i * FIELDS : (i + 1) * FIELDS, i * TILE : (i + 1) * TILE
            ]


def near_kernel(n_lon, start_sweep, *refs):
    half = n_lon // 2
    lon = lax.axis_index("lon")
    targets_ref, moved_ref, x_refs, refs = refs[0], refs[1], refs[2 : 2 + half], refs[2 + half :]
    if start_sweep:
        pq_hbm, w_hbm, acc_ref, w_ref, far_ref, lon_ref, lat_ref, pq_ref, sems = refs
        mine = lon & half
        near = pltpu.make_async_copy(w_hbm.at[pl.ds(mine, half)], w_ref, sems.at[0])
        parts = pltpu.make_async_copy(pq_hbm.at[pl.ds(1, 2)], pq_ref, sems.at[1])
        far = pltpu.make_async_copy(w_hbm.at[pl.ds(half - mine, half)], far_ref, sems.at[2])
        for copy in (near, parts, far):
            copy.start()
    else:
        w_ref, acc_ref = refs
    acc_ref[...] = moved_ref[0 : acc_ref.shape[0], :]
    if start_sweep:
        near.wait()
    for r, x_ref in enumerate(x_refs):
        add_source(lon ^ r, (lon ^ r) & (half - 1), targets_ref, x_ref, w_ref, acc_ref)
    if start_sweep:
        parts.wait()
        to_tiles(pq_ref.at[0], lon_ref)
        to_tiles(pq_ref.at[1], lat_ref)
        far.wait()


def far_kernel(n_lat, n_lon, start_sweep, *refs):
    half = n_lon // 2
    targets_ref, coef_ref, moved_ref, w_ref = refs[:4]
    x_refs, refs = refs[4 : 4 + half], refs[4 + half :]
    if start_sweep:
        monitor_ref, balance_ref, pay_ref, acc_ref = refs
    else:
        det_ref, monitor_ref, balance_ref, pay_ref, acc_ref = refs
    rows, cols = monitor_ref.shape
    blocks = cols // TILE
    acc_ref[...] = jnp.zeros_like(acc_ref)
    here = lax.axis_index("lon")
    for r, x_ref in zip(range(half, n_lon), x_refs):
        add_source(here ^ r, (here ^ r) & (half - 1), targets_ref, x_ref, w_ref, acc_ref)

    field_id = lax.broadcasted_iota(jnp.int32, (FIELDS, TILE), 0)
    coef = jnp.zeros((FIELDS, TILE), jnp.float32)
    for f in range(FIELDS):
        coef = jnp.where(field_id == f, coef_ref[f], coef)
    for b in range(rows // 8):
        for c in range(blocks):
            parts = []
            for i in range(8):
                start = ((b * 8 + i) * blocks + c) * FIELDS
                place = slice(start, start + FIELDS)
                blended = moved_ref[place, :] + acc_ref[place, :]
                parts.append(coef * (blended * blended))
            monitor_ref[b * 8 : b * 8 + 8, c * TILE : (c + 1) * TILE] = jnp.sqrt(
                1.0 + sum_fields(parts)
            )

    monitor = monitor_ref[...]
    if start_sweep:
        det = jnp.ones((rows, cols), jnp.float32)
        balance = monitor
    else:
        det = det_ref[...]
        balance = monitor * det
    balance_ref[...] = balance
    inverse = 1.0 / monitor
    count = rows * cols
    mean = jnp.sum(jnp.sum(balance, axis=0, keepdims=True), axis=1, keepdims=True) / count
    away = balance - mean
    squares = jnp.sum(jnp.sum(away * away, axis=0, keepdims=True), axis=1, keepdims=True)
    lane_id = lax.broadcasted_iota(jnp.int32, (1, TILE), 1)
    stats = jnp.where(lane_id == 0, mean, jnp.where(lane_id == 1, squares, 0.0))
    stat_at = cols if start_sweep else 2 * cols
    for j in range(n_lat * n_lon):
        pay_ref[j, :, stat_at : stat_at + TILE] = stats

    lat, lon = mesh_place()
    left = lax.rem(lon + n_lon - 1, n_lon)
    right = lax.rem(lon + 1, n_lon)
    for side, col in ((left, 0), (right, cols - 1)):
        lanes = column_to_lanes(det[:, col : col + 1], 0)
        lanes = lanes + column_to_lanes(inverse[:, col : col + 1], rows)
        pay_ref[lat * n_lon + side, :, 0:TILE] = lanes

    def send_row(other, row):
        pay_ref[other * n_lon + lon, :, stat_at - cols : stat_at] = inverse[row : row + 1, :]
        if not start_sweep:
            pay_ref[other * n_lon + lon, :, 0:cols] = det[row : row + 1, :]
        for side, col in ((left, 0), (right, cols - 1)):
            lanes = jnp.where(
                lane_id == 0,
                det[row : row + 1, col : col + 1],
                inverse[row : row + 1, col : col + 1],
            )
            pay_ref[other * n_lon + side, :, 0:TILE] = lanes

    @pl.when(lat > 0)
    def _():
        send_row(lat - 1, 0)

    @pl.when(lat < n_lat - 1)
    def _():
        send_row(lat + 1, rows - 1)


def whole_stats(got_ref, n_dev, count, stat_at):
    total = got_ref[0, :, stat_at : stat_at + TILE]
    for j in range(1, n_dev):
        total = total + got_ref[j, :, stat_at : stat_at + TILE]
    target = lane_value(total, 0) / n_dev
    apart = jnp.zeros((1, TILE), jnp.float32)
    for j in range(n_dev):
        away = got_ref[j, :, stat_at : stat_at + TILE] - target
        apart = apart + away * away
    variance = (lane_value(total, 1) / count + lane_value(apart, 0)) / n_dev
    return target, jnp.sqrt(variance + 1e-06)


def update_kernel(n_lat, n_lon, n_got, *refs):
    place_ref = refs[0]
    got_refs = refs[1 : 1 + n_got]
    refs = refs[1 + n_got :]
    if n_got > 1:
        old_ref, refs = refs[0], refs[1:]
    monitor_ref, balance_ref, still_ref, lon_ref, lat_ref = refs[:5]
    pot_ref, det_ref, moved_ref = refs[5:8]
    send_refs, (zonal_ref, meridional_ref) = refs[8:-2], refs[-2:]
    rows, cols = monitor_ref.shape
    blocks = cols // TILE
    n_dev = n_lat * n_lon
    lat, lon = mesh_place()
    left = lax.rem(lon + n_lon - 1, n_lon)
    right = lax.rem(lon + 1, n_lon)
    below = jnp.maximum(lat - 1, 0)
    above = jnp.minimum(lat + 1, n_lat - 1)

    south_row = jnp.zeros((1, cols), jnp.float32)
    north_row = jnp.zeros((1, cols), jnp.float32)
    sides = [jnp.zeros((rows, 1), jnp.float32)] * 2
    corners = [jnp.zeros((1, 1), jnp.float32)] * 4
    for order, got_ref in enumerate(got_refs):
        stat_at = 2 * cols if order else cols
        target, spread = whole_stats(got_ref, n_dev, rows * cols, stat_at)

        def gain(det, inverse):
            return 0.5 * (det - target * inverse) / spread

        def row_from(j):
            det = got_ref[j, :, 0:cols] if stat_at > cols else 1.0
            return gain(det, got_ref[j, :, stat_at - cols : stat_at])

        south_row = south_row + row_from(below * n_lon + lon)
        north_row = north_row + row_from(above * n_lon + lon)
        for i, side in enumerate((left, right)):
            lanes = got_ref[lat * n_lon + side, :, 0:TILE]
            sides[i] = sides[i] + gain(
                lanes_to_column(lanes, rows, 0), lanes_to_column(lanes, rows, rows)
            )
        for i, (other, side) in enumerate(
            ((below, left), (below, right), (above, left), (above, right))
        ):
            lanes = got_ref[other * n_lon + side, :, 0:TILE]
            corners[i] = corners[i] + gain(lane_value(lanes, 0), lane_value(lanes, 1))

    has_south, has_north = lat > 0, lat < n_lat - 1
    south_row = jnp.where(has_south, south_row, 0.0)
    north_row = jnp.where(has_north, north_row, 0.0)
    corners = [
        jnp.where(has, corner, 0.0)
        for has, corner in zip((has_south, has_south, has_north, has_north), corners)
    ]

    potential = 0.5 * (balance_ref[...] - target) / (monitor_ref[...] * spread)
    if n_got > 1:
        potential = old_ref[...] + potential
    pot_ref[...] = potential

    row_id = lax.broadcasted_iota(jnp.int32, (rows, cols), 0)
    lane_id = lax.broadcasted_iota(jnp.int32, (rows, cols), 1)
    first, last = row_id == 0, row_id == rows - 1
    west_edge, east_edge = lane_id == 0, lane_id == cols - 1
    north = jnp.where(last, north_row, pltpu.roll(potential, rows - 1, 0))
    south = jnp.where(first, south_row, pltpu.roll(potential, 1, 0))
    east = jnp.where(east_edge, sides[1], pltpu.roll(potential, cols - 1, 1))
    west = jnp.where(west_edge, sides[0], pltpu.roll(potential, 1, 1))
    tall = north - south
    zonal_ref[...] = (east - west) * 0.5
    meridional_ref[...] = tall * 0.5

    for r in range(rows):
        for c in range(blocks):
            lanes = slice(c * TILE, (c + 1) * TILE)
            start = (r * blocks + c) * FIELDS
            place = slice(start, start + FIELDS)
            zonal = jnp.broadcast_to(zonal_ref[r : r + 1, lanes], (FIELDS, TILE))
            meridional = jnp.broadcast_to(meridional_ref[r : r + 1, lanes], (FIELDS, TILE))
            moved_ref[place, :] = (
                still_ref[place, :]
                + zonal * lon_ref[place, :]
                + meridional * lat_ref[place, :]
            )
    zero_tile(moved_ref)
    pack_tiles(lon, place_ref, moved_ref, send_refs)

    small_row = lax.broadcasted_iota(jnp.int32, (rows, TILE), 0)

    def side_tall(column, low, high):
        wide = jnp.broadcast_to(column, (rows, TILE))
        up = jnp.where(small_row == rows - 1, high, pltpu.roll(wide, rows - 1, 0))
        down = jnp.where(small_row == 0, low, pltpu.roll(wide, 1, 0))
        return (up - down)[:, 0:1]

    west_tall = side_tall(sides[0], corners[0], corners[2])
    east_tall = side_tall(sides[1], corners[1], corners[3])
    tall_east = jnp.where(east_edge, east_tall, pltpu.roll(tall, cols - 1, 1))
    tall_west = jnp.where(west_edge, west_tall, pltpu.roll(tall, 1, 1))
    mixed = (tall_east - tall_west) * 0.25
    second_lon = east - 2.0 * potential + west
    second_lat = north - 2.0 * potential + south
    det_ref[...] = (1.0 + second_lon) * (1.0 + second_lat) - mixed * mixed


def last_kernel(n_dev, got_ref, old_ref, monitor_ref, balance_ref, pot_ref, scaled_ref):
    rows, cols = monitor_ref.shape
    target, spread = whole_stats(got_ref, n_dev, rows * cols, 0)
    residual = balance_ref[...] - target
    scaled_ref[...] = residual / spread
    pot_ref[...] = old_ref[...] + 0.5 * residual / (monitor_ref[...] * spread)


def per_device(pq, coef, departing, occupancy, arriving, blocks_w):
    n_lat, n_lon = lax.axis_size("lat"), lax.axis_size("lon")
    n_dev = n_lat * n_lon
    rows, cols = pq.shape[2:]
    ids = departing[0, 0]
    occ = occupancy[0, 0]
    targets = arriving[0, 0]
    weights = blocks_w[0, 0]
    smem = pl.BlockSpec(memory_space=SMEM)
    vmem = pl.BlockSpec(memory_space=VMEM)
    hbm = pl.BlockSpec(memory_space=pltpu.MemorySpace.HBM)
    f32 = jnp.float32
    grid = jax.ShapeDtypeStruct((rows, cols), f32)
    half = n_lon // 2
    tile_rows = FIELDS * rows * cols // TILE
    acc_shape = jax.ShapeDtypeStruct((tile_rows, TILE), f32)
    moved_shape = jax.ShapeDtypeStruct((tile_rows + FIELDS, TILE), f32)
    send_shape = jax.ShapeDtypeStruct((CAP * FIELDS, TILE), jnp.bfloat16)
    half_shape = VMEM((half, CAP, TILE, TILE), weights.dtype)
    params = pltpu.CompilerParams(vmem_limit_bytes=5 << 20)
    near_cost = pl.CostEstimate(
        flops=2 * half * CAP * FIELDS * TILE * TILE,
        bytes_accessed=2 * half * CAP * TILE * TILE,
        transcendentals=0,
    )

    def in_hbm(array):
        return pltpu.with_memory_space_constraint(array, pltpu.MemorySpace.HBM)

    still, places, targets, coef, *send = pl.pallas_call(
        functools.partial(first_kernel, n_lon),
        out_shape=(
            moved_shape,
            jax.ShapeDtypeStruct(ids.shape, ids.dtype),
            jax.ShapeDtypeStruct(targets.shape, targets.dtype),
            jax.ShapeDtypeStruct(coef.shape, coef.dtype),
        )
        + (send_shape,) * n_lon,
        in_specs=[hbm] * 5,
        out_specs=(vmem,) * (4 + n_lon),
        scratch_shapes=[
            pltpu.VMEM(ids.shape, jnp.int32),
            pltpu.SMEM(occ.shape, jnp.int32),
            pltpu.SMEM(ids.shape, jnp.int32),
            pltpu.VMEM(pq.shape[1:], pq.dtype),
            pltpu.SemaphoreType.DMA((5,)),
        ],
        compiler_params=params,
        name="first",
    )(*[in_hbm(x) for x in (ids, occ, targets, coef, pq)])

    def interp(send, moved, det, kept):
        got = list(send)
        for r in reversed(range(1, n_lon)):
            got[r] = lax.ppermute(send[r], "lon", [(i, i ^ r) for i in range(n_lon)])
        start_sweep = det is None
        if start_sweep:
            args = [in_hbm(pq), in_hbm(weights)]
            out_shape = (acc_shape, half_shape, half_shape, acc_shape, acc_shape)
            scratch = [
                pltpu.VMEM((2,) + pq.shape[1:], pq.dtype),
                pltpu.SemaphoreType.DMA((3,)),
            ]
        else:
            args, out_shape, scratch = [kept[0]], (acc_shape,), []
        base, *fetched = pl.pallas_call(
            functools.partial(near_kernel, n_lon, start_sweep),
            out_shape=out_shape,
            in_specs=[smem] + [vmem] * (1 + half) + [hbm if start_sweep else vmem] * len(args),
            out_specs=(vmem,) * len(out_shape),
            scratch_shapes=scratch,
            compiler_params=params,
            cost_estimate=near_cost,
            name="near",
        )(targets, moved, *got[:half], *args)
        kept = fetched if start_sweep else kept
        pay_width = TILE + (cols if start_sweep else 2 * cols)
        out_shape = (grid, grid, jax.ShapeDtypeStruct((n_dev, 1, pay_width), f32))
        args = [targets, coef, base, kept[1], *got[half:]] + ([] if start_sweep else [det])
        outs = pl.pallas_call(
            functools.partial(far_kernel, n_lat, n_lon, start_sweep),
            out_shape=out_shape,
            in_specs=[smem, smem] + [vmem] * (len(args) - 2),
            out_specs=(vmem,) * 3,
            scratch_shapes=[pltpu.VMEM((tile_rows, TILE), f32)],
            compiler_params=params,
            name="far",
        )(*args)
        return (*outs, kept)

    def share(pay):
        return lax.all_to_all(pay, ("lat", "lon"), 0, 0, tiled=True)

    gots = []
    moved = still
    potential = det = kept = None
    for sweep in range(SWEEPS):
        monitor, balance, pay, kept = interp(send, moved, det, kept)
        if sweep == SWEEPS - 1:
            break
        gots.append(share(pay))
        olds = [] if potential is None else [potential]
        args = [places, *gots, *olds, monitor, balance, still, *kept[2:]]
        potential, det, moved, *send = pl.pallas_call(
            functools.partial(update_kernel, n_lat, n_lon, len(gots)),
            out_shape=(grid, grid, moved_shape) + (send_shape,) * n_lon,
            in_specs=[smem] + [vmem] * (len(args) - 1),
            out_specs=(vmem,) * (3 + n_lon),
            scratch_shapes=[pltpu.VMEM((rows, cols), f32)] * 2,
            compiler_params=params,
            name="update",
        )(*args)

    got = share(pay[:, :, pay.shape[2] - TILE :])
    return pl.pallas_call(
        functools.partial(last_kernel, n_dev),
        out_shape=(grid, grid),
        in_specs=[vmem] * 4,
        out_specs=(vmem, vmem),
        compiler_params=params,
        name="last",
    )(got, potential, monitor, balance)


def solution(mesh):
    in_specs = (
        P(None, None, "lat", "lon"),
        P(),
        P("lat", "lon", None, None),
        P("lat", "lon", None),
        P("lat", "lon", None, None),
        P("lat", "lon", None, None, None, None),
    )
    out_specs = (P("lat", "lon"), P("lat", "lon"))
    return jax.shard_map(
        per_device, mesh=mesh, in_specs=in_specs, out_specs=out_specs, check_vma=False
    )
```

```python
import functools

import jax
import jax.numpy as jnp
from jax import lax
from jax.experimental import pallas as pl
from jax.experimental.pallas import tpu as pltpu
from jax.sharding import PartitionSpec as P


FIELDS = 8
TILE = 128
CAP = 32
SWEEPS = 3


VMEM = pltpu.MemorySpace.VMEM
SMEM = pltpu.MemorySpace.SMEM


def to_tiles(pq_ref, out_ref):
    fields, rows, cols = pq_ref.shape
    blocks = cols // TILE
    for b in range(rows // 16):
        for c in range(blocks):
            part = pq_ref[:, b * 16 : b * 16 + 16, c * TILE : (c + 1) * TILE]
            part = jnp.transpose(part.astype(jnp.float32), (1, 0, 2))
            for i in range(16):
                start = ((b * 16 + i) * blocks + c) * fields
                out_ref[start : start + fields, :] = part[i]


def pack_tiles(lon, rows_ref, moved_ref, send_refs):
    for r, send_ref in enumerate(send_refs):
        dest = lon ^ r
        for k in range(0, CAP, 2):
            pair = []
            for i in (k, k + 1):
                start = pl.multiple_of(rows_ref[dest, i], FIELDS)
                pair.append(moved_ref[pl.ds(start, FIELDS), :])
            send_ref[k * FIELDS : (k + 2) * FIELDS, :] = jnp.concatenate(pair, axis=0).astype(
                jnp.bfloat16
            )


def zero_tile(moved_ref):
    moved_ref[moved_ref.shape[0] - FIELDS :, :] = jnp.zeros((FIELDS, TILE), jnp.float32)


def first_kernel(n_lon, *refs):
    ids_hbm, occ_hbm, targets_hbm, coef_hbm, pq_hbm = refs[:5]
    still_ref, rows_ref, targets_ref, coef_ref = refs[5:9]
    send_refs, (ids_ref, occ_ref, place_ref, pq_ref, sems) = refs[9:-5], refs[-5:]
    fields = pltpu.make_async_copy(pq_hbm.at[0], pq_ref, sems.at[0])
    lists = [
        pltpu.make_async_copy(ids_hbm, ids_ref, sems.at[1]),
        pltpu.make_async_copy(occ_hbm, occ_ref, sems.at[2]),
    ]
    later = [
        pltpu.make_async_copy(targets_hbm, targets_ref, sems.at[3]),
        pltpu.make_async_copy(coef_hbm, coef_ref, sems.at[4]),
    ]
    for copy in (*lists, fields, *later):
        copy.start()
    zero_tile(still_ref)
    for copy in lists:
        copy.wait()
    dest_id = lax.broadcasted_iota(jnp.int32, (n_lon, CAP), 0)
    slot_id = lax.broadcasted_iota(jnp.int32, (n_lon, CAP), 1)
    count = jnp.zeros((n_lon, CAP), jnp.int32)
    for d in range(n_lon):
        count = jnp.where(dest_id == d, occ_ref[d], count)
    zero_row = still_ref.shape[0] - FIELDS
    rows_ref[...] = jnp.where(slot_id < count, ids_ref[...] * FIELDS, zero_row)
    places = pltpu.make_async_copy(rows_ref, place_ref, sems.at[1])
    places.start()
    fields.wait()
    to_tiles(pq_ref, still_ref)
    places.wait()
    pack_tiles(lax.axis_index("lon"), place_ref, still_ref, send_refs)
    for copy in later:
        copy.wait()


def sum_fields(tiles):
    sub = lax.broadcasted_iota(jnp.int32, (8, TILE), 0)
    high = (sub & 4) == 0
    pairs = []
    for i in range(4):
        one, two = tiles[i], tiles[i + 4]
        kept, moving = jnp.where(high, one, two), jnp.where(high, two, one)
        pairs.append(kept + pltpu.roll(moving, 4, 0))
    for step in (2, 1):
        near = (sub & step) == 0
        pairs = [
            jnp.where(
                near,
                pairs[i] + pltpu.roll(pairs[i], 8 - step, 0),
                pairs[i + step] + pltpu.roll(pairs[i + step], step, 0),
            )
            for i in range(step)
        ]
    return pairs[0]


def column_to_lanes(column, offset):
    rows = column.shape[0]
    row_id = lax.broadcasted_iota(jnp.int32, (rows, TILE), 0)
    lane_id = lax.broadcasted_iota(jnp.int32, (rows, TILE), 1)
    wide = jnp.broadcast_to(column, (rows, TILE))
    return jnp.sum(jnp.where(lane_id == row_id + offset, wide, 0.0), axis=0, keepdims=True)


def lanes_to_column(lanes, rows, offset):
    row_id = lax.broadcasted_iota(jnp.int32, (rows, TILE), 0)
    lane_id = lax.broadcasted_iota(jnp.int32, (rows, TILE), 1)
    wide = jnp.broadcast_to(lanes, (rows, TILE))
    return jnp.sum(jnp.where(lane_id == row_id + offset, wide, 0.0), axis=1, keepdims=True)


def lane_value(lanes, index):
    lane_id = lax.broadcasted_iota(jnp.int32, lanes.shape, 1)
    return jnp.sum(jnp.where(lane_id == index, lanes, 0.0), axis=1, keepdims=True)


def mesh_place():
    lat, lon = lax.axis_index("lat"), lax.axis_index("lon")
    return lat, lon


def add_source(source, local, targets_ref, x_ref, w_ref, acc_ref):
    for k in range(0, CAP, 2):
        pair = jnp.concatenate([w_ref[local, k], w_ref[local, k + 1]], axis=1)
        out = jnp.dot(
            x_ref[k * FIELDS : (k + 2) * FIELDS, :], pair, preferred_element_type=jnp.float32
        )
        for i in (0, 1):
            start = pl.multiple_of(targets_ref[source, k + i] * FIELDS, FIELDS)
            acc_ref[pl.ds(start, FIELDS), :] += out[
                i * FIELDS : (i + 1) * FIELDS, i * TILE : (i + 1) * TILE
            ]


def groups(n_lon):
    half = n_lon // 2
    late = list(range(2, half)) + list(range(half, half + half // 2))
    return [r for r in [0, 1] + list(range(n_lon - 1, half - 1, -1)) if r not in late], late


def add_sources(n_lon, partners, targets_ref, x_refs, near_ref, far_ref, acc_ref):
    half = n_lon // 2
    lon = lax.axis_index("lon")
    for r, x_ref in zip(partners, x_refs):
        w_ref = near_ref if r < half else far_ref
        add_source(lon ^ r, (lon ^ r) & (half - 1), targets_ref, x_ref, w_ref, acc_ref)


def early_kernel(n_lon, start_sweep, *refs):
    half = n_lon // 2
    partners = groups(n_lon)[0]
    count = len(partners)
    targets_ref, moved_ref, x_refs, refs = refs[0], refs[1], refs[2 : 2 + count], refs[2 + count :]
    if start_sweep:
        pq_hbm, w_hbm, acc_ref, near_ref, far_ref, lon_ref, lat_ref, pq_ref, sems = refs
        mine = lax.axis_index("lon") & half
        far = pltpu.make_async_copy(w_hbm.at[pl.ds(half - mine, half)], far_ref, sems.at[0])
        near = pltpu.make_async_copy(w_hbm.at[pl.ds(mine, half)], near_ref, sems.at[1])
        parts = pltpu.make_async_copy(pq_hbm.at[pl.ds(1, 2)], pq_ref, sems.at[2])
        for copy in (parts, far, near):
            copy.start()
    else:
        near_ref, far_ref, acc_ref = refs
    acc_ref[...] = moved_ref[0 : acc_ref.shape[0], :]
    if start_sweep:
        parts.wait()
        to_tiles(pq_ref.at[0], lon_ref)
        to_tiles(pq_ref.at[1], lat_ref)
        far.wait()
        near.wait()
    add_sources(n_lon, partners, targets_ref, x_refs, near_ref, far_ref, acc_ref)


def late_kernel(n_lat, n_lon, start_sweep, *refs):
    partners = groups(n_lon)[1]
    count = len(partners)
    targets_ref, coef_ref, moved_ref, near_ref, far_ref = refs[:5]
    x_refs, refs = refs[5 : 5 + count], refs[5 + count :]
    if start_sweep:
        monitor_ref, balance_ref, pay_ref, acc_ref = refs
    else:
        det_ref, monitor_ref, balance_ref, pay_ref, acc_ref = refs
    rows, cols = monitor_ref.shape
    blocks = cols // TILE
    acc_ref[...] = jnp.zeros_like(acc_ref)
    add_sources(n_lon, partners, targets_ref, x_refs, near_ref, far_ref, acc_ref)

    field_id = lax.broadcasted_iota(jnp.int32, (FIELDS, TILE), 0)
    coef = jnp.zeros((FIELDS, TILE), jnp.float32)
    for f in range(FIELDS):
        coef = jnp.where(field_id == f, coef_ref[f], coef)
    for b in range(rows // 8):
        for c in range(blocks):
            parts = []
            for i in range(8):
                start = ((b * 8 + i) * blocks + c) * FIELDS
                place = slice(start, start + FIELDS)
                blended = moved_ref[place, :] + acc_ref[place, :]
                parts.append(coef * (blended * blended))
            monitor_ref[b * 8 : b * 8 + 8, c * TILE : (c + 1) * TILE] = jnp.sqrt(
                1.0 + sum_fields(parts)
            )

    monitor = monitor_ref[...]
    if start_sweep:
        det = jnp.ones((rows, cols), jnp.float32)
        balance = monitor
    else:
        det = det_ref[...]
        balance = monitor * det
    balance_ref[...] = balance
    inverse = 1.0 / monitor
    count = rows * cols
    mean = jnp.sum(jnp.sum(balance, axis=0, keepdims=True), axis=1, keepdims=True) / count
    away = balance - mean
    squares = jnp.sum(jnp.sum(away * away, axis=0, keepdims=True), axis=1, keepdims=True)
    lane_id = lax.broadcasted_iota(jnp.int32, (1, TILE), 1)
    stats = jnp.where(lane_id == 0, mean, jnp.where(lane_id == 1, squares, 0.0))
    stat_at = cols if start_sweep else 2 * cols
    for j in range(n_lat * n_lon):
        pay_ref[j, :, stat_at : stat_at + TILE] = stats

    lat, lon = mesh_place()
    left = lax.rem(lon + n_lon - 1, n_lon)
    right = lax.rem(lon + 1, n_lon)
    for side, col in ((left, 0), (right, cols - 1)):
        lanes = column_to_lanes(det[:, col : col + 1], 0)
        lanes = lanes + column_to_lanes(inverse[:, col : col + 1], rows)
        pay_ref[lat * n_lon + side, :, 0:TILE] = lanes

    def send_row(other, row):
        pay_ref[other * n_lon + lon, :, stat_at - cols : stat_at] = inverse[row : row + 1, :]
        if not start_sweep:
            pay_ref[other * n_lon + lon, :, 0:cols] = det[row : row + 1, :]
        for side, col in ((left, 0), (right, cols - 1)):
            lanes = jnp.where(
                lane_id == 0,
                det[row : row + 1, col : col + 1],
                inverse[row : row + 1, col : col + 1],
            )
            pay_ref[other * n_lon + side, :, 0:TILE] = lanes

    @pl.when(lat > 0)
    def _():
        send_row(lat - 1, 0)

    @pl.when(lat < n_lat - 1)
    def _():
        send_row(lat + 1, rows - 1)


def whole_stats(got_ref, n_dev, count, stat_at):
    total = got_ref[0, :, stat_at : stat_at + TILE]
    for j in range(1, n_dev):
        total = total + got_ref[j, :, stat_at : stat_at + TILE]
    target = lane_value(total, 0) / n_dev
    apart = jnp.zeros((1, TILE), jnp.float32)
    for j in range(n_dev):
        away = got_ref[j, :, stat_at : stat_at + TILE] - target
        apart = apart + away * away
    variance = (lane_value(total, 1) / count + lane_value(apart, 0)) / n_dev
    return target, jnp.sqrt(variance + 1e-06)


def update_kernel(n_lat, n_lon, n_got, *refs):
    place_ref = refs[0]
    got_refs = refs[1 : 1 + n_got]
    refs = refs[1 + n_got :]
    if n_got > 1:
        old_ref, refs = refs[0], refs[1:]
    monitor_ref, balance_ref, still_ref, lon_ref, lat_ref = refs[:5]
    pot_ref, det_ref, moved_ref = refs[5:8]
    send_refs, (zonal_ref, meridional_ref) = refs[8:-2], refs[-2:]
    rows, cols = monitor_ref.shape
    blocks = cols // TILE
    n_dev = n_lat * n_lon
    lat, lon = mesh_place()
    left = lax.rem(lon + n_lon - 1, n_lon)
    right = lax.rem(lon + 1, n_lon)
    below = jnp.maximum(lat - 1, 0)
    above = jnp.minimum(lat + 1, n_lat - 1)

    south_row = jnp.zeros((1, cols), jnp.float32)
    north_row = jnp.zeros((1, cols), jnp.float32)
    sides = [jnp.zeros((rows, 1), jnp.float32)] * 2
    corners = [jnp.zeros((1, 1), jnp.float32)] * 4
    for order, got_ref in enumerate(got_refs):
        stat_at = 2 * cols if order else cols
        target, spread = whole_stats(got_ref, n_dev, rows * cols, stat_at)

        def gain(det, inverse):
            return 0.5 * (det - target * inverse) / spread

        def row_from(j):
            det = got_ref[j, :, 0:cols] if stat_at > cols else 1.0
            return gain(det, got_ref[j, :, stat_at - cols : stat_at])

        south_row = south_row + row_from(below * n_lon + lon)
        north_row = north_row + row_from(above * n_lon + lon)
        for i, side in enumerate((left, right)):
            lanes = got_ref[lat * n_lon + side, :, 0:TILE]
            sides[i] = sides[i] + gain(
                lanes_to_column(lanes, rows, 0), lanes_to_column(lanes, rows, rows)
            )
        for i, (other, side) in enumerate(
            ((below, left), (below, right), (above, left), (above, right))
        ):
            lanes = got_ref[other * n_lon + side, :, 0:TILE]
            corners[i] = corners[i] + gain(lane_value(lanes, 0), lane_value(lanes, 1))

    has_south, has_north = lat > 0, lat < n_lat - 1
    south_row = jnp.where(has_south, south_row, 0.0)
    north_row = jnp.where(has_north, north_row, 0.0)
    corners = [
        jnp.where(has, corner, 0.0)
        for has, corner in zip((has_south, has_south, has_north, has_north), corners)
    ]

    potential = 0.5 * (balance_ref[...] - target) / (monitor_ref[...] * spread)
    if n_got > 1:
        potential = old_ref[...] + potential
    pot_ref[...] = potential

    row_id = lax.broadcasted_iota(jnp.int32, (rows, cols), 0)
    lane_id = lax.broadcasted_iota(jnp.int32, (rows, cols), 1)
    first, last = row_id == 0, row_id == rows - 1
    west_edge, east_edge = lane_id == 0, lane_id == cols - 1
    north = jnp.where(last, north_row, pltpu.roll(potential, rows - 1, 0))
    south = jnp.where(first, south_row, pltpu.roll(potential, 1, 0))
    east = jnp.where(east_edge, sides[1], pltpu.roll(potential, cols - 1, 1))
    west = jnp.where(west_edge, sides[0], pltpu.roll(potential, 1, 1))
    tall = north - south
    zonal_ref[...] = (east - west) * 0.5
    meridional_ref[...] = tall * 0.5

    for r in range(rows):
        for c in range(blocks):
            lanes = slice(c * TILE, (c + 1) * TILE)
            start = (r * blocks + c) * FIELDS
            place = slice(start, start + FIELDS)
            zonal = jnp.broadcast_to(zonal_ref[r : r + 1, lanes], (FIELDS, TILE))
            meridional = jnp.broadcast_to(meridional_ref[r : r + 1, lanes], (FIELDS, TILE))
            moved_ref[place, :] = (
                still_ref[place, :]
                + zonal * lon_ref[place, :]
                + meridional * lat_ref[place, :]
            )
    zero_tile(moved_ref)
    pack_tiles(lon, place_ref, moved_ref, send_refs)

    small_row = lax.broadcasted_iota(jnp.int32, (rows, TILE), 0)

    def side_tall(column, low, high):
        wide = jnp.broadcast_to(column, (rows, TILE))
        up = jnp.where(small_row == rows - 1, high, pltpu.roll(wide, rows - 1, 0))
        down = jnp.where(small_row == 0, low, pltpu.roll(wide, 1, 0))
        return (up - down)[:, 0:1]

    west_tall = side_tall(sides[0], corners[0], corners[2])
    east_tall = side_tall(sides[1], corners[1], corners[3])
    tall_east = jnp.where(east_edge, east_tall, pltpu.roll(tall, cols - 1, 1))
    tall_west = jnp.where(west_edge, west_tall, pltpu.roll(tall, 1, 1))
    mixed = (tall_east - tall_west) * 0.25
    second_lon = east - 2.0 * potential + west
    second_lat = north - 2.0 * potential + south
    det_ref[...] = (1.0 + second_lon) * (1.0 + second_lat) - mixed * mixed


def last_kernel(n_dev, got_ref, old_ref, monitor_ref, balance_ref, pot_ref, scaled_ref):
    rows, cols = monitor_ref.shape
    target, spread = whole_stats(got_ref, n_dev, rows * cols, 0)
    residual = balance_ref[...] - target
    scaled_ref[...] = residual / spread
    pot_ref[...] = old_ref[...] + 0.5 * residual / (monitor_ref[...] * spread)


def per_device(pq, coef, departing, occupancy, arriving, blocks_w):
    n_lat, n_lon = lax.axis_size("lat"), lax.axis_size("lon")
    n_dev = n_lat * n_lon
    rows, cols = pq.shape[2:]
    ids = departing[0, 0]
    occ = occupancy[0, 0]
    targets = arriving[0, 0]
    weights = blocks_w[0, 0]
    smem = pl.BlockSpec(memory_space=SMEM)
    vmem = pl.BlockSpec(memory_space=VMEM)
    hbm = pl.BlockSpec(memory_space=pltpu.MemorySpace.HBM)
    f32 = jnp.float32
    grid = jax.ShapeDtypeStruct((rows, cols), f32)
    half = n_lon // 2
    tile_rows = FIELDS * rows * cols // TILE
    acc_shape = jax.ShapeDtypeStruct((tile_rows, TILE), f32)
    moved_shape = jax.ShapeDtypeStruct((tile_rows + FIELDS, TILE), f32)
    send_shape = jax.ShapeDtypeStruct((CAP * FIELDS, TILE), jnp.bfloat16)
    half_shape = VMEM((half, CAP, TILE, TILE), weights.dtype)
    params = pltpu.CompilerParams(vmem_limit_bytes=5 << 20)
    early_cost = pl.CostEstimate(
        flops=2 * half * CAP * FIELDS * TILE * TILE,
        bytes_accessed=2 * half * CAP * TILE * TILE,
        transcendentals=0,
    )

    def in_hbm(array):
        return pltpu.with_memory_space_constraint(array, pltpu.MemorySpace.HBM)

    still, places, targets, coef, *send = pl.pallas_call(
        functools.partial(first_kernel, n_lon),
        out_shape=(
            moved_shape,
            jax.ShapeDtypeStruct(ids.shape, ids.dtype),
            jax.ShapeDtypeStruct(targets.shape, targets.dtype),
            jax.ShapeDtypeStruct(coef.shape, coef.dtype),
        )
        + (send_shape,) * n_lon,
        in_specs=[hbm] * 5,
        out_specs=(vmem,) * (4 + n_lon),
        scratch_shapes=[
            pltpu.VMEM(ids.shape, jnp.int32),
            pltpu.SMEM(occ.shape, jnp.int32),
            pltpu.SMEM(ids.shape, jnp.int32),
            pltpu.VMEM(pq.shape[1:], pq.dtype),
            pltpu.SemaphoreType.DMA((5,)),
        ],
        compiler_params=params,
        name="first",
    )(*[in_hbm(x) for x in (ids, occ, targets, coef, pq)])

    def interp(send, moved, det, kept):
        got = list(send)
        for r in range(1, n_lon):
            got[r] = lax.ppermute(send[r], "lon", [(i, i ^ r) for i in range(n_lon)])
        early, late = ([got[r] for r in group] for group in groups(n_lon))
        start_sweep = det is None
        if start_sweep:
            args = [in_hbm(pq), in_hbm(weights)]
            out_shape = (acc_shape, half_shape, half_shape, acc_shape, acc_shape)
            scratch = [
                pltpu.VMEM((2,) + pq.shape[1:], pq.dtype),
                pltpu.SemaphoreType.DMA((3,)),
            ]
        else:
            args, out_shape, scratch = list(kept[:2]), (acc_shape,), []
        base, *fetched = pl.pallas_call(
            functools.partial(early_kernel, n_lon, start_sweep),
            out_shape=out_shape,
            in_specs=[smem]
            + [vmem] * (1 + len(early))
            + [hbm if start_sweep else vmem] * len(args),
            out_specs=(vmem,) * len(out_shape),
            scratch_shapes=scratch,
            compiler_params=params,
            cost_estimate=early_cost,
            name="early",
        )(targets, moved, *early, *args)
        kept = fetched if start_sweep else kept
        pay_width = TILE + (cols if start_sweep else 2 * cols)
        out_shape = (grid, grid, jax.ShapeDtypeStruct((n_dev, 1, pay_width), f32))
        args = [targets, coef, base, *kept[:2], *late] + ([] if start_sweep else [det])
        outs = pl.pallas_call(
            functools.partial(late_kernel, n_lat, n_lon, start_sweep),
            out_shape=out_shape,
            in_specs=[smem, smem] + [vmem] * (len(args) - 2),
            out_specs=(vmem,) * 3,
            scratch_shapes=[pltpu.VMEM((tile_rows, TILE), f32)],
            compiler_params=params,
            name="late",
        )(*args)
        return (*outs, kept)

    def share(pay):
        return lax.all_to_all(pay, ("lat", "lon"), 0, 0, tiled=True)

    gots = []
    moved = still
    potential = det = kept = None
    for sweep in range(SWEEPS):
        monitor, balance, pay, kept = interp(send, moved, det, kept)
        if sweep == SWEEPS - 1:
            break
        gots.append(share(pay))
        olds = [] if potential is None else [potential]
        args = [places, *gots, *olds, monitor, balance, still, *kept[2:]]
        potential, det, moved, *send = pl.pallas_call(
            functools.partial(update_kernel, n_lat, n_lon, len(gots)),
            out_shape=(grid, grid, moved_shape) + (send_shape,) * n_lon,
            in_specs=[smem] + [vmem] * (len(args) - 1),
            out_specs=(vmem,) * (3 + n_lon),
            scratch_shapes=[pltpu.VMEM((rows, cols), f32)] * 2,
            compiler_params=params,
            name="update",
        )(*args)

    got = share(pay[:, :, pay.shape[2] - TILE :])
    return pl.pallas_call(
        functools.partial(last_kernel, n_dev),
        out_shape=(grid, grid),
        in_specs=[vmem] * 4,
        out_specs=(vmem, vmem),
        compiler_params=params,
        name="last",
    )(got, potential, monitor, balance)


def solution(mesh):
    in_specs = (
        P(None, None, "lat", "lon"),
        P(),
        P("lat", "lon", None, None),
        P("lat", "lon", None),
        P("lat", "lon", None, None),
        P("lat", "lon", None, None, None, None),
    )
    out_specs = (P("lat", "lon"), P("lat", "lon"))
    return jax.shard_map(
        per_device, mesh=mesh, in_specs=in_specs, out_specs=out_specs, check_vma=False
    )
```

```python
import functools

import jax
import jax.numpy as jnp
from jax import lax
from jax.experimental import pallas as pl
from jax.experimental.pallas import tpu as pltpu
from jax.sharding import PartitionSpec as P


FIELDS = 8
TILE = 128
CAP = 32
SWEEPS = 3


VMEM = pltpu.MemorySpace.VMEM
SMEM = pltpu.MemorySpace.SMEM


def to_tiles(pq_ref, out_ref):
    fields, rows, cols = pq_ref.shape
    blocks = cols // TILE
    for b in range(rows // 16):
        for c in range(blocks):
            part = pq_ref[:, b * 16 : b * 16 + 16, c * TILE : (c + 1) * TILE]
            part = jnp.transpose(part.astype(jnp.float32), (1, 0, 2))
            for i in range(16):
                start = ((b * 16 + i) * blocks + c) * fields
                out_ref[start : start + fields, :] = part[i]


def pack_tiles(lon, rows_ref, moved_ref, send_refs):
    for r, send_ref in enumerate(send_refs):
        dest = lon ^ r
        for k in range(0, CAP, 2):
            pair = []
            for i in (k, k + 1):
                start = pl.multiple_of(rows_ref[dest, i], FIELDS)
                pair.append(moved_ref[pl.ds(start, FIELDS), :])
            send_ref[k * FIELDS : (k + 2) * FIELDS, :] = jnp.concatenate(pair, axis=0).astype(
                jnp.bfloat16
            )


def zero_tile(moved_ref):
    moved_ref[moved_ref.shape[0] - FIELDS :, :] = jnp.zeros((FIELDS, TILE), jnp.float32)


def first_kernel(n_lon, *refs):
    ids_hbm, occ_hbm, targets_hbm, coef_hbm, pq_hbm = refs[:5]
    still_ref, rows_ref, targets_ref, coef_ref = refs[5:9]
    send_refs, (ids_ref, occ_ref, place_ref, pq_ref, sems) = refs[9:-5], refs[-5:]
    fields = pltpu.make_async_copy(pq_hbm.at[0], pq_ref, sems.at[0])
    lists = [
        pltpu.make_async_copy(ids_hbm, ids_ref, sems.at[1]),
        pltpu.make_async_copy(occ_hbm, occ_ref, sems.at[2]),
    ]
    later = [
        pltpu.make_async_copy(targets_hbm, targets_ref, sems.at[3]),
        pltpu.make_async_copy(coef_hbm, coef_ref, sems.at[4]),
    ]
    for copy in (*lists, fields, *later):
        copy.start()
    zero_tile(still_ref)
    for copy in lists:
        copy.wait()
    dest_id = lax.broadcasted_iota(jnp.int32, (n_lon, CAP), 0)
    slot_id = lax.broadcasted_iota(jnp.int32, (n_lon, CAP), 1)
    count = jnp.zeros((n_lon, CAP), jnp.int32)
    for d in range(n_lon):
        count = jnp.where(dest_id == d, occ_ref[d], count)
    zero_row = still_ref.shape[0] - FIELDS
    rows_ref[...] = jnp.where(slot_id < count, ids_ref[...] * FIELDS, zero_row)
    places = pltpu.make_async_copy(rows_ref, place_ref, sems.at[1])
    places.start()
    fields.wait()
    to_tiles(pq_ref, still_ref)
    places.wait()
    pack_tiles(lax.axis_index("lon"), place_ref, still_ref, send_refs)
    for copy in later:
        copy.wait()


def sum_fields(tiles):
    sub = lax.broadcasted_iota(jnp.int32, (8, TILE), 0)
    high = (sub & 4) == 0
    pairs = []
    for i in range(4):
        one, two = tiles[i], tiles[i + 4]
        kept, moving = jnp.where(high, one, two), jnp.where(high, two, one)
        pairs.append(kept + pltpu.roll(moving, 4, 0))
    for step in (2, 1):
        near = (sub & step) == 0
        pairs = [
            jnp.where(
                near,
                pairs[i] + pltpu.roll(pairs[i], 8 - step, 0),
                pairs[i + step] + pltpu.roll(pairs[i + step], step, 0),
            )
            for i in range(step)
        ]
    return pairs[0]


def column_to_lanes(column, offset):
    rows = column.shape[0]
    row_id = lax.broadcasted_iota(jnp.int32, (rows, TILE), 0)
    lane_id = lax.broadcasted_iota(jnp.int32, (rows, TILE), 1)
    wide = jnp.broadcast_to(column, (rows, TILE))
    return jnp.sum(jnp.where(lane_id == row_id + offset, wide, 0.0), axis=0, keepdims=True)


def lanes_to_column(lanes, rows, offset):
    row_id = lax.broadcasted_iota(jnp.int32, (rows, TILE), 0)
    lane_id = lax.broadcasted_iota(jnp.int32, (rows, TILE), 1)
    wide = jnp.broadcast_to(lanes, (rows, TILE))
    return jnp.sum(jnp.where(lane_id == row_id + offset, wide, 0.0), axis=1, keepdims=True)


def lane_value(lanes, index):
    lane_id = lax.broadcasted_iota(jnp.int32, lanes.shape, 1)
    return jnp.sum(jnp.where(lane_id == index, lanes, 0.0), axis=1, keepdims=True)


def mesh_place():
    lat, lon = lax.axis_index("lat"), lax.axis_index("lon")
    return lat, lon


def add_source(source, local, targets_ref, x_ref, w_ref, acc_ref):
    for k in range(0, CAP, 2):
        pair = jnp.concatenate([w_ref[local, k], w_ref[local, k + 1]], axis=1)
        out = jnp.dot(
            x_ref[k * FIELDS : (k + 2) * FIELDS, :], pair, preferred_element_type=jnp.float32
        )
        for i in (0, 1):
            start = pl.multiple_of(targets_ref[source, k + i] * FIELDS, FIELDS)
            acc_ref[pl.ds(start, FIELDS), :] += out[
                i * FIELDS : (i + 1) * FIELDS, i * TILE : (i + 1) * TILE
            ]


def groups(n_lon):
    half = n_lon // 2
    late = list(range(2, half)) + list(range(half, half + half // 2))
    return [r for r in [0, 1] + list(range(n_lon - 1, half - 1, -1)) if r not in late], late


def add_sources(n_lon, partners, targets_ref, x_refs, near_ref, far_ref, acc_ref):
    half = n_lon // 2
    lon = lax.axis_index("lon")
    for r, x_ref in zip(partners, x_refs):
        w_ref = near_ref if r < half else far_ref
        add_source(lon ^ r, (lon ^ r) & (half - 1), targets_ref, x_ref, w_ref, acc_ref)


def fetch_kernel(n_lon, *refs):
    pq_hbm, w_hbm, near_ref, far_ref, lon_ref, lat_ref, pq_ref, sems = refs
    half = n_lon // 2
    mine = lax.axis_index("lon") & half
    far = pltpu.make_async_copy(w_hbm.at[pl.ds(half - mine, half)], far_ref, sems.at[0])
    near = pltpu.make_async_copy(w_hbm.at[pl.ds(mine, half)], near_ref, sems.at[1])
    parts = pltpu.make_async_copy(pq_hbm.at[pl.ds(1, 2)], pq_ref, sems.at[2])
    for copy in (parts, far, near):
        copy.start()
    parts.wait()
    to_tiles(pq_ref.at[0], lon_ref)
    to_tiles(pq_ref.at[1], lat_ref)
    far.wait()
    near.wait()


def early_kernel(n_lon, *refs):
    targets_ref, moved_ref, near_ref, far_ref = refs[:4]
    x_refs, acc_ref = refs[4:-1], refs[-1]
    acc_ref[...] = moved_ref[0 : acc_ref.shape[0], :]
    add_sources(n_lon, groups(n_lon)[0], targets_ref, x_refs, near_ref, far_ref, acc_ref)


def late_kernel(n_lat, n_lon, start_sweep, *refs):
    partners = groups(n_lon)[1]
    count = len(partners)
    targets_ref, coef_ref, _, near_ref, far_ref = refs[:5]
    x_refs, refs = refs[5 : 5 + count], refs[5 + count :]
    if start_sweep:
        monitor_ref, balance_ref, pay_ref, acc_ref = refs
    else:
        det_ref, monitor_ref, balance_ref, pay_ref, acc_ref = refs
    rows, cols = monitor_ref.shape
    blocks = cols // TILE
    add_sources(n_lon, partners, targets_ref, x_refs, near_ref, far_ref, acc_ref)

    field_id = lax.broadcasted_iota(jnp.int32, (FIELDS, TILE), 0)
    coef = jnp.zeros((FIELDS, TILE), jnp.float32)
    for f in range(FIELDS):
        coef = jnp.where(field_id == f, coef_ref[f], coef)
    for b in range(rows // 8):
        for c in range(blocks):
            parts = []
            for i in range(8):
                start = ((b * 8 + i) * blocks + c) * FIELDS
                place = slice(start, start + FIELDS)
                blended = acc_ref[place, :]
                parts.append(coef * (blended * blended))
            monitor_ref[b * 8 : b * 8 + 8, c * TILE : (c + 1) * TILE] = jnp.sqrt(
                1.0 + sum_fields(parts)
            )

    monitor = monitor_ref[...]
    if start_sweep:
        det = jnp.ones((rows, cols), jnp.float32)
        balance = monitor
    else:
        det = det_ref[...]
        balance = monitor * det
    balance_ref[...] = balance
    inverse = 1.0 / monitor
    count = rows * cols
    mean = jnp.sum(jnp.sum(balance, axis=0, keepdims=True), axis=1, keepdims=True) / count
    away = balance - mean
    squares = jnp.sum(jnp.sum(away * away, axis=0, keepdims=True), axis=1, keepdims=True)
    lane_id = lax.broadcasted_iota(jnp.int32, (1, TILE), 1)
    stats = jnp.where(lane_id == 0, mean, jnp.where(lane_id == 1, squares, 0.0))
    stat_at = cols if start_sweep else 2 * cols
    for j in range(n_lat * n_lon):
        pay_ref[j, :, stat_at : stat_at + TILE] = stats

    lat, lon = mesh_place()
    left = lax.rem(lon + n_lon - 1, n_lon)
    right = lax.rem(lon + 1, n_lon)
    for side, col in ((left, 0), (right, cols - 1)):
        lanes = column_to_lanes(det[:, col : col + 1], 0)
        lanes = lanes + column_to_lanes(inverse[:, col : col + 1], rows)
        pay_ref[lat * n_lon + side, :, 0:TILE] = lanes

    def send_row(other, row):
        pay_ref[other * n_lon + lon, :, stat_at - cols : stat_at] = inverse[row : row + 1, :]
        if not start_sweep:
            pay_ref[other * n_lon + lon, :, 0:cols] = det[row : row + 1, :]
        for side, col in ((left, 0), (right, cols - 1)):
            lanes = jnp.where(
                lane_id == 0,
                det[row : row + 1, col : col + 1],
                inverse[row : row + 1, col : col + 1],
            )
            pay_ref[other * n_lon + side, :, 0:TILE] = lanes

    @pl.when(lat > 0)
    def _():
        send_row(lat - 1, 0)

    @pl.when(lat < n_lat - 1)
    def _():
        send_row(lat + 1, rows - 1)


def whole_stats(got_ref, n_dev, count, stat_at):
    total = got_ref[0, :, stat_at : stat_at + TILE]
    for j in range(1, n_dev):
        total = total + got_ref[j, :, stat_at : stat_at + TILE]
    target = lane_value(total, 0) / n_dev
    apart = jnp.zeros((1, TILE), jnp.float32)
    for j in range(n_dev):
        away = got_ref[j, :, stat_at : stat_at + TILE] - target
        apart = apart + away * away
    variance = (lane_value(total, 1) / count + lane_value(apart, 0)) / n_dev
    return target, jnp.sqrt(variance + 1e-06)


def update_kernel(n_lat, n_lon, n_got, *refs):
    place_ref = refs[0]
    got_refs = refs[1 : 1 + n_got]
    refs = refs[1 + n_got :]
    if n_got > 1:
        old_ref, refs = refs[0], refs[1:]
    monitor_ref, balance_ref, still_ref, lon_ref, lat_ref = refs[:5]
    pot_ref, det_ref, moved_ref = refs[5:8]
    send_refs, (zonal_ref, meridional_ref) = refs[8:-2], refs[-2:]
    rows, cols = monitor_ref.shape
    blocks = cols // TILE
    n_dev = n_lat * n_lon
    lat, lon = mesh_place()
    left = lax.rem(lon + n_lon - 1, n_lon)
    right = lax.rem(lon + 1, n_lon)
    below = jnp.maximum(lat - 1, 0)
    above = jnp.minimum(lat + 1, n_lat - 1)

    south_row = jnp.zeros((1, cols), jnp.float32)
    north_row = jnp.zeros((1, cols), jnp.float32)
    sides = [jnp.zeros((rows, 1), jnp.float32)] * 2
    corners = [jnp.zeros((1, 1), jnp.float32)] * 4
    for order, got_ref in enumerate(got_refs):
        stat_at = 2 * cols if order else cols
        target, spread = whole_stats(got_ref, n_dev, rows * cols, stat_at)

        def gain(det, inverse):
            return 0.5 * (det - target * inverse) / spread

        def row_from(j):
            det = got_ref[j, :, 0:cols] if stat_at > cols else 1.0
            return gain(det, got_ref[j, :, stat_at - cols : stat_at])

        south_row = south_row + row_from(below * n_lon + lon)
        north_row = north_row + row_from(above * n_lon + lon)
        for i, side in enumerate((left, right)):
            lanes = got_ref[lat * n_lon + side, :, 0:TILE]
            sides[i] = sides[i] + gain(
                lanes_to_column(lanes, rows, 0), lanes_to_column(lanes, rows, rows)
            )
        for i, (other, side) in enumerate(
            ((below, left), (below, right), (above, left), (above, right))
        ):
            lanes = got_ref[other * n_lon + side, :, 0:TILE]
            corners[i] = corners[i] + gain(lane_value(lanes, 0), lane_value(lanes, 1))

    has_south, has_north = lat > 0, lat < n_lat - 1
    south_row = jnp.where(has_south, south_row, 0.0)
    north_row = jnp.where(has_north, north_row, 0.0)
    corners = [
        jnp.where(has, corner, 0.0)
        for has, corner in zip((has_south, has_south, has_north, has_north), corners)
    ]

    potential = 0.5 * (balance_ref[...] - target) / (monitor_ref[...] * spread)
    if n_got > 1:
        potential = old_ref[...] + potential
    pot_ref[...] = potential

    row_id = lax.broadcasted_iota(jnp.int32, (rows, cols), 0)
    lane_id = lax.broadcasted_iota(jnp.int32, (rows, cols), 1)
    first, last = row_id == 0, row_id == rows - 1
    west_edge, east_edge = lane_id == 0, lane_id == cols - 1
    north = jnp.where(last, north_row, pltpu.roll(potential, rows - 1, 0))
    south = jnp.where(first, south_row, pltpu.roll(potential, 1, 0))
    east = jnp.where(east_edge, sides[1], pltpu.roll(potential, cols - 1, 1))
    west = jnp.where(west_edge, sides[0], pltpu.roll(potential, 1, 1))
    tall = north - south
    zonal_ref[...] = (east - west) * 0.5
    meridional_ref[...] = tall * 0.5

    for r in range(rows):
        for c in range(blocks):
            lanes = slice(c * TILE, (c + 1) * TILE)
            start = (r * blocks + c) * FIELDS
            place = slice(start, start + FIELDS)
            zonal = jnp.broadcast_to(zonal_ref[r : r + 1, lanes], (FIELDS, TILE))
            meridional = jnp.broadcast_to(meridional_ref[r : r + 1, lanes], (FIELDS, TILE))
            moved_ref[place, :] = (
                still_ref[place, :]
                + zonal * lon_ref[place, :]
                + meridional * lat_ref[place, :]
            )
    zero_tile(moved_ref)
    pack_tiles(lon, place_ref, moved_ref, send_refs)

    small_row = lax.broadcasted_iota(jnp.int32, (rows, TILE), 0)

    def side_tall(column, low, high):
        wide = jnp.broadcast_to(column, (rows, TILE))
        up = jnp.where(small_row == rows - 1, high, pltpu.roll(wide, rows - 1, 0))
        down = jnp.where(small_row == 0, low, pltpu.roll(wide, 1, 0))
        return (up - down)[:, 0:1]

    west_tall = side_tall(sides[0], corners[0], corners[2])
    east_tall = side_tall(sides[1], corners[1], corners[3])
    tall_east = jnp.where(east_edge, east_tall, pltpu.roll(tall, cols - 1, 1))
    tall_west = jnp.where(west_edge, west_tall, pltpu.roll(tall, 1, 1))
    mixed = (tall_east - tall_west) * 0.25
    second_lon = east - 2.0 * potential + west
    second_lat = north - 2.0 * potential + south
    det_ref[...] = (1.0 + second_lon) * (1.0 + second_lat) - mixed * mixed


def last_kernel(n_dev, got_ref, old_ref, monitor_ref, balance_ref, pot_ref, scaled_ref):
    rows, cols = monitor_ref.shape
    target, spread = whole_stats(got_ref, n_dev, rows * cols, 0)
    residual = balance_ref[...] - target
    scaled_ref[...] = residual / spread
    pot_ref[...] = old_ref[...] + 0.5 * residual / (monitor_ref[...] * spread)


def per_device(pq, coef, departing, occupancy, arriving, blocks_w):
    n_lat, n_lon = lax.axis_size("lat"), lax.axis_size("lon")
    n_dev = n_lat * n_lon
    rows, cols = pq.shape[2:]
    ids = departing[0, 0]
    occ = occupancy[0, 0]
    targets = arriving[0, 0]
    weights = blocks_w[0, 0]
    smem = pl.BlockSpec(memory_space=SMEM)
    vmem = pl.BlockSpec(memory_space=VMEM)
    hbm = pl.BlockSpec(memory_space=pltpu.MemorySpace.HBM)
    f32 = jnp.float32
    grid = jax.ShapeDtypeStruct((rows, cols), f32)
    half = n_lon // 2
    tile_rows = FIELDS * rows * cols // TILE
    acc_shape = jax.ShapeDtypeStruct((tile_rows, TILE), f32)
    moved_shape = jax.ShapeDtypeStruct((tile_rows + FIELDS, TILE), f32)
    send_shape = jax.ShapeDtypeStruct((CAP * FIELDS, TILE), jnp.bfloat16)
    half_shape = VMEM((half, CAP, TILE, TILE), weights.dtype)
    params = pltpu.CompilerParams(vmem_limit_bytes=5 << 20)
    early_cost = pl.CostEstimate(
        flops=2 * half * CAP * FIELDS * TILE * TILE,
        bytes_accessed=2 * half * CAP * TILE * TILE,
        transcendentals=0,
    )

    def in_hbm(array):
        return pltpu.with_memory_space_constraint(array, pltpu.MemorySpace.HBM)

    still, places, targets, coef, *send = pl.pallas_call(
        functools.partial(first_kernel, n_lon),
        out_shape=(
            moved_shape,
            jax.ShapeDtypeStruct(ids.shape, ids.dtype),
            jax.ShapeDtypeStruct(targets.shape, targets.dtype),
            jax.ShapeDtypeStruct(coef.shape, coef.dtype),
        )
        + (send_shape,) * n_lon,
        in_specs=[hbm] * 5,
        out_specs=(vmem,) * (4 + n_lon),
        scratch_shapes=[
            pltpu.VMEM(ids.shape, jnp.int32),
            pltpu.SMEM(occ.shape, jnp.int32),
            pltpu.SMEM(ids.shape, jnp.int32),
            pltpu.VMEM(pq.shape[1:], pq.dtype),
            pltpu.SemaphoreType.DMA((5,)),
        ],
        compiler_params=params,
        name="first",
    )(*[in_hbm(x) for x in (ids, occ, targets, coef, pq)])

    def interp(send, moved, det, kept):
        got = list(send)
        for r in range(1, n_lon):
            got[r] = lax.ppermute(send[r], "lon", [(i, i ^ r) for i in range(n_lon)])
        early, late = ([got[r] for r in group] for group in groups(n_lon))
        start_sweep = det is None
        if start_sweep:
            kept = pl.pallas_call(
                functools.partial(fetch_kernel, n_lon),
                out_shape=(half_shape, half_shape, acc_shape, acc_shape),
                in_specs=[hbm] * 2,
                out_specs=(vmem,) * 4,
                scratch_shapes=[
                    pltpu.VMEM((2,) + pq.shape[1:], pq.dtype),
                    pltpu.SemaphoreType.DMA((3,)),
                ],
                compiler_params=params,
                cost_estimate=pl.CostEstimate(
                    flops=1 << 20, bytes_accessed=10 << 20, transcendentals=0
                ),
                name="fetch",
            )(in_hbm(pq), in_hbm(weights))
        base = pl.pallas_call(
            functools.partial(early_kernel, n_lon),
            out_shape=acc_shape,
            in_specs=[smem] + [vmem] * (3 + len(early)),
            out_specs=vmem,
            compiler_params=params,
            cost_estimate=early_cost,
            name="early",
        )(targets, moved, *kept[:2], *early)
        pay_width = TILE + (cols if start_sweep else 2 * cols)
        out_shape = (grid, grid, jax.ShapeDtypeStruct((n_dev, 1, pay_width), f32), acc_shape)
        args = [targets, coef, base, *kept[:2], *late] + ([] if start_sweep else [det])
        outs = pl.pallas_call(
            functools.partial(late_kernel, n_lat, n_lon, start_sweep),
            out_shape=out_shape,
            in_specs=[smem, smem] + [vmem] * (len(args) - 2),
            out_specs=(vmem,) * 4,
            input_output_aliases={2: 3},
            compiler_params=params,
            name="late",
        )(*args)
        outs = outs[:3]
        return (*outs, kept)

    def share(pay):
        return lax.all_to_all(pay, ("lat", "lon"), 0, 0, tiled=True)

    gots = []
    moved = still
    potential = det = kept = None
    for sweep in range(SWEEPS):
        monitor, balance, pay, kept = interp(send, moved, det, kept)
        if sweep == SWEEPS - 1:
            break
        gots.append(share(pay))
        olds = [] if potential is None else [potential]
        args = [places, *gots, *olds, monitor, balance, still, *kept[2:]]
        potential, det, moved, *send = pl.pallas_call(
            functools.partial(update_kernel, n_lat, n_lon, len(gots)),
            out_shape=(grid, grid, moved_shape) + (send_shape,) * n_lon,
            in_specs=[smem] + [vmem] * (len(args) - 1),
            out_specs=(vmem,) * (3 + n_lon),
            scratch_shapes=[pltpu.VMEM((rows, cols), f32)] * 2,
            compiler_params=params,
            name="update",
        )(*args)

    got = share(pay[:, :, pay.shape[2] - TILE :])
    return pl.pallas_call(
        functools.partial(last_kernel, n_dev),
        out_shape=(grid, grid),
        in_specs=[vmem] * 4,
        out_specs=(vmem, vmem),
        compiler_params=params,
        name="last",
    )(got, potential, monitor, balance)


def solution(mesh):
    in_specs = (
        P(None, None, "lat", "lon"),
        P(),
        P("lat", "lon", None, None),
        P("lat", "lon", None),
        P("lat", "lon", None, None),
        P("lat", "lon", None, None, None, None),
    )
    out_specs = (P("lat", "lon"), P("lat", "lon"))
    return jax.shard_map(
        per_device, mesh=mesh, in_specs=in_specs, out_specs=out_specs, check_vma=False
    )
```

```python
import functools

import jax
import jax.numpy as jnp
from jax import lax
from jax.experimental import pallas as pl
from jax.experimental.pallas import tpu as pltpu
from jax.sharding import PartitionSpec as P


FIELDS = 8
TILE = 128
CAP = 32
SWEEPS = 3


VMEM = pltpu.MemorySpace.VMEM
SMEM = pltpu.MemorySpace.SMEM


def to_tiles(pq_ref, out_ref):
    fields, rows, cols = pq_ref.shape
    blocks = cols // TILE
    for b in range(rows // 16):
        for c in range(blocks):
            part = pq_ref[:, b * 16 : b * 16 + 16, c * TILE : (c + 1) * TILE]
            part = jnp.transpose(part.astype(jnp.float32), (1, 0, 2))
            for i in range(16):
                start = ((b * 16 + i) * blocks + c) * fields
                out_ref[start : start + fields, :] = part[i]


def pack_tiles(lon, rows_ref, moved_ref, send_refs):
    for r, send_ref in enumerate(send_refs):
        dest = lon ^ r
        for k in range(0, CAP, 2):
            pair = []
            for i in (k, k + 1):
                start = pl.multiple_of(rows_ref[dest, i], FIELDS)
                pair.append(moved_ref[pl.ds(start, FIELDS), :])
            send_ref[k * FIELDS : (k + 2) * FIELDS, :] = jnp.concatenate(pair, axis=0).astype(
                jnp.bfloat16
            )


def zero_tile(moved_ref):
    moved_ref[moved_ref.shape[0] - FIELDS :, :] = jnp.zeros((FIELDS, TILE), jnp.float32)


def first_kernel(n_lon, *refs):
    ids_hbm, occ_hbm, targets_hbm, coef_hbm, pq_hbm = refs[:5]
    still_ref, rows_ref, targets_ref, coef_ref = refs[5:9]
    send_refs, (ids_ref, occ_ref, place_ref, pq_ref, sems) = refs[9:-5], refs[-5:]
    fields = pltpu.make_async_copy(pq_hbm.at[0], pq_ref, sems.at[0])
    lists = [
        pltpu.make_async_copy(ids_hbm, ids_ref, sems.at[1]),
        pltpu.make_async_copy(occ_hbm, occ_ref, sems.at[2]),
    ]
    later = [
        pltpu.make_async_copy(targets_hbm, targets_ref, sems.at[3]),
        pltpu.make_async_copy(coef_hbm, coef_ref, sems.at[4]),
    ]
    for copy in (*lists, fields, *later):
        copy.start()
    zero_tile(still_ref)
    for copy in lists:
        copy.wait()
    dest_id = lax.broadcasted_iota(jnp.int32, (n_lon, CAP), 0)
    slot_id = lax.broadcasted_iota(jnp.int32, (n_lon, CAP), 1)
    count = jnp.zeros((n_lon, CAP), jnp.int32)
    for d in range(n_lon):
        count = jnp.where(dest_id == d, occ_ref[d], count)
    zero_row = still_ref.shape[0] - FIELDS
    rows_ref[...] = jnp.where(slot_id < count, ids_ref[...] * FIELDS, zero_row)
    places = pltpu.make_async_copy(rows_ref, place_ref, sems.at[1])
    places.start()
    fields.wait()
    to_tiles(pq_ref, still_ref)
    places.wait()
    pack_tiles(lax.axis_index("lon"), place_ref, still_ref, send_refs)
    for copy in later:
        copy.wait()


def sum_fields(tiles):
    sub = lax.broadcasted_iota(jnp.int32, (8, TILE), 0)
    high = (sub & 4) == 0
    pairs = []
    for i in range(4):
        one, two = tiles[i], tiles[i + 4]
        kept, moving = jnp.where(high, one, two), jnp.where(high, two, one)
        pairs.append(kept + pltpu.roll(moving, 4, 0))
    for step in (2, 1):
        near = (sub & step) == 0
        pairs = [
            jnp.where(
                near,
                pairs[i] + pltpu.roll(pairs[i], 8 - step, 0),
                pairs[i + step] + pltpu.roll(pairs[i + step], step, 0),
            )
            for i in range(step)
        ]
    return pairs[0]


def column_to_lanes(column, offset):
    rows = column.shape[0]
    row_id = lax.broadcasted_iota(jnp.int32, (rows, TILE), 0)
    lane_id = lax.broadcasted_iota(jnp.int32, (rows, TILE), 1)
    wide = jnp.broadcast_to(column, (rows, TILE))
    return jnp.sum(jnp.where(lane_id == row_id + offset, wide, 0.0), axis=0, keepdims=True)


def lanes_to_column(lanes, rows, offset):
    row_id = lax.broadcasted_iota(jnp.int32, (rows, TILE), 0)
    lane_id = lax.broadcasted_iota(jnp.int32, (rows, TILE), 1)
    wide = jnp.broadcast_to(lanes, (rows, TILE))
    return jnp.sum(jnp.where(lane_id == row_id + offset, wide, 0.0), axis=1, keepdims=True)


def lane_value(lanes, index):
    lane_id = lax.broadcasted_iota(jnp.int32, lanes.shape, 1)
    return jnp.sum(jnp.where(lane_id == index, lanes, 0.0), axis=1, keepdims=True)


def mesh_place():
    lat, lon = lax.axis_index("lat"), lax.axis_index("lon")
    return lat, lon


def add_source(source, local, targets_ref, x_ref, w_ref, acc_ref):
    for k in range(0, CAP, 2):
        pair = jnp.concatenate([w_ref[local, k], w_ref[local, k + 1]], axis=1)
        out = jnp.dot(
            x_ref[k * FIELDS : (k + 2) * FIELDS, :], pair, preferred_element_type=jnp.float32
        )
        for i in (0, 1):
            start = pl.multiple_of(targets_ref[source, k + i] * FIELDS, FIELDS)
            acc_ref[pl.ds(start, FIELDS), :] += out[
                i * FIELDS : (i + 1) * FIELDS, i * TILE : (i + 1) * TILE
            ]


def groups(n_lon):
    half = n_lon // 2
    late = list(range(2, half)) + list(range(half, half + half // 2))
    return [r for r in [0, 1] + list(range(n_lon - 1, half - 1, -1)) if r not in late], late


def add_sources(n_lon, partners, targets_ref, x_refs, near_ref, far_ref, acc_ref):
    half = n_lon // 2
    lon = lax.axis_index("lon")
    for r, x_ref in zip(partners, x_refs):
        w_ref = near_ref if r < half else far_ref
        add_source(lon ^ r, (lon ^ r) & (half - 1), targets_ref, x_ref, w_ref, acc_ref)


def fetch_kernel(n_lon, *refs):
    pq_hbm, w_hbm, near_ref, far_ref, lon_ref, lat_ref, pq_ref, sems = refs
    half = n_lon // 2
    mine = lax.axis_index("lon") & half
    far = pltpu.make_async_copy(w_hbm.at[pl.ds(half - mine, half)], far_ref, sems.at[0])
    near = pltpu.make_async_copy(w_hbm.at[pl.ds(mine, half)], near_ref, sems.at[1])
    parts = pltpu.make_async_copy(pq_hbm.at[pl.ds(1, 2)], pq_ref, sems.at[2])
    for copy in (parts, far, near):
        copy.start()
    parts.wait()
    to_tiles(pq_ref.at[0], lon_ref)
    to_tiles(pq_ref.at[1], lat_ref)
    far.wait()
    near.wait()


def early_kernel(n_lon, *refs):
    targets_ref, moved_ref, near_ref, far_ref = refs[:4]
    x_refs, acc_ref = refs[4:-1], refs[-1]
    acc_ref[...] = moved_ref[0 : acc_ref.shape[0], :]
    add_sources(n_lon, groups(n_lon)[0], targets_ref, x_refs, near_ref, far_ref, acc_ref)


def late_kernel(n_lat, n_lon, start_sweep, *refs):
    partners = groups(n_lon)[1]
    count = len(partners)
    targets_ref, coef_ref, _, near_ref, far_ref = refs[:5]
    x_refs, refs = refs[5 : 5 + count], refs[5 + count :]
    if start_sweep:
        monitor_ref, balance_ref, pay_ref, acc_ref = refs
    else:
        det_ref, monitor_ref, balance_ref, pay_ref, acc_ref = refs
    rows, cols = monitor_ref.shape
    blocks = cols // TILE
    add_sources(n_lon, partners, targets_ref, x_refs, near_ref, far_ref, acc_ref)

    field_id = lax.broadcasted_iota(jnp.int32, (FIELDS, TILE), 0)
    coef = jnp.zeros((FIELDS, TILE), jnp.float32)
    for f in range(FIELDS):
        coef = jnp.where(field_id == f, coef_ref[f], coef)
    for b in range(rows // 8):
        for c in range(blocks):
            parts = []
            for i in range(8):
                start = ((b * 8 + i) * blocks + c) * FIELDS
                place = slice(start, start + FIELDS)
                blended = acc_ref[place, :]
                parts.append(coef * (blended * blended))
            monitor_ref[b * 8 : b * 8 + 8, c * TILE : (c + 1) * TILE] = jnp.sqrt(
                1.0 + sum_fields(parts)
            )

    monitor = monitor_ref[...]
    if start_sweep:
        det = jnp.ones((rows, cols), jnp.float32)
        balance = monitor
    else:
        det = det_ref[...]
        balance = monitor * det
    balance_ref[...] = balance
    inverse = 1.0 / monitor
    count = rows * cols
    mean = jnp.sum(jnp.sum(balance, axis=0, keepdims=True), axis=1, keepdims=True) / count
    away = balance - mean
    squares = jnp.sum(jnp.sum(away * away, axis=0, keepdims=True), axis=1, keepdims=True)
    lane_id = lax.broadcasted_iota(jnp.int32, (1, TILE), 1)
    stats = jnp.where(lane_id == 0, mean, jnp.where(lane_id == 1, squares, 0.0))
    stat_at = cols if start_sweep else 2 * cols
    for j in range(n_lat * n_lon):
        pay_ref[j, :, stat_at : stat_at + TILE] = stats

    lat, lon = mesh_place()
    left = lax.rem(lon + n_lon - 1, n_lon)
    right = lax.rem(lon + 1, n_lon)
    for side, col in ((left, 0), (right, cols - 1)):
        lanes = column_to_lanes(det[:, col : col + 1], 0)
        lanes = lanes + column_to_lanes(inverse[:, col : col + 1], rows)
        pay_ref[lat * n_lon + side, :, 0:TILE] = lanes

    def send_row(other, row):
        pay_ref[other * n_lon + lon, :, stat_at - cols : stat_at] = inverse[row : row + 1, :]
        if not start_sweep:
            pay_ref[other * n_lon + lon, :, 0:cols] = det[row : row + 1, :]
        for side, col in ((left, 0), (right, cols - 1)):
            lanes = jnp.where(
                lane_id == 0,
                det[row : row + 1, col : col + 1],
                inverse[row : row + 1, col : col + 1],
            )
            pay_ref[other * n_lon + side, :, 0:TILE] = lanes

    @pl.when(lat > 0)
    def _():
        send_row(lat - 1, 0)

    @pl.when(lat < n_lat - 1)
    def _():
        send_row(lat + 1, rows - 1)


def whole_stats(got_ref, n_dev, count, stat_at):
    total = got_ref[0, :, stat_at : stat_at + TILE]
    for j in range(1, n_dev):
        total = total + got_ref[j, :, stat_at : stat_at + TILE]
    centre = total / n_dev
    apart = jnp.zeros((1, TILE), jnp.float32)
    for j in range(n_dev):
        away = got_ref[j, :, stat_at : stat_at + TILE] - centre
        apart = apart + away * away
    target = lane_value(centre, 0)
    variance = (lane_value(total, 1) / count + lane_value(apart, 0)) / n_dev
    return target, jnp.sqrt(variance + 1e-06)


def update_kernel(n_lat, n_lon, n_got, *refs):
    place_ref = refs[0]
    got_refs = refs[1 : 1 + n_got]
    refs = refs[1 + n_got :]
    if n_got > 1:
        old_ref, refs = refs[0], refs[1:]
    monitor_ref, balance_ref, still_ref, lon_ref, lat_ref = refs[:5]
    pot_ref, det_ref, moved_ref = refs[5:8]
    send_refs, (zonal_ref, meridional_ref) = refs[8:-2], refs[-2:]
    rows, cols = monitor_ref.shape
    blocks = cols // TILE
    n_dev = n_lat * n_lon
    lat, lon = mesh_place()
    left = lax.rem(lon + n_lon - 1, n_lon)
    right = lax.rem(lon + 1, n_lon)
    below = jnp.maximum(lat - 1, 0)
    above = jnp.minimum(lat + 1, n_lat - 1)

    south_row = jnp.zeros((1, cols), jnp.float32)
    north_row = jnp.zeros((1, cols), jnp.float32)
    sides = [jnp.zeros((rows, 1), jnp.float32)] * 2
    corners = [jnp.zeros((1, 1), jnp.float32)] * 4
    for order, got_ref in enumerate(got_refs):
        stat_at = 2 * cols if order else cols
        target, spread = whole_stats(got_ref, n_dev, rows * cols, stat_at)

        def gain(det, inverse):
            return 0.5 * (det - target * inverse) / spread

        def row_from(j):
            det = got_ref[j, :, 0:cols] if stat_at > cols else 1.0
            return gain(det, got_ref[j, :, stat_at - cols : stat_at])

        south_row = south_row + row_from(below * n_lon + lon)
        north_row = north_row + row_from(above * n_lon + lon)
        for i, side in enumerate((left, right)):
            lanes = got_ref[lat * n_lon + side, :, 0:TILE]
            sides[i] = sides[i] + gain(
                lanes_to_column(lanes, rows, 0), lanes_to_column(lanes, rows, rows)
            )
        for i, (other, side) in enumerate(
            ((below, left), (below, right), (above, left), (above, right))
        ):
            lanes = got_ref[other * n_lon + side, :, 0:TILE]
            corners[i] = corners[i] + gain(lane_value(lanes, 0), lane_value(lanes, 1))

    has_south, has_north = lat > 0, lat < n_lat - 1
    south_row = jnp.where(has_south, south_row, 0.0)
    north_row = jnp.where(has_north, north_row, 0.0)
    corners = [
        jnp.where(has, corner, 0.0)
        for has, corner in zip((has_south, has_south, has_north, has_north), corners)
    ]

    potential = 0.5 * (balance_ref[...] - target) / (monitor_ref[...] * spread)
    if n_got > 1:
        potential = old_ref[...] + potential
    pot_ref[...] = potential

    row_id = lax.broadcasted_iota(jnp.int32, (rows, cols), 0)
    lane_id = lax.broadcasted_iota(jnp.int32, (rows, cols), 1)
    first, last = row_id == 0, row_id == rows - 1
    west_edge, east_edge = lane_id == 0, lane_id == cols - 1
    north = jnp.where(last, north_row, pltpu.roll(potential, rows - 1, 0))
    south = jnp.where(first, south_row, pltpu.roll(potential, 1, 0))
    east = jnp.where(east_edge, sides[1], pltpu.roll(potential, cols - 1, 1))
    west = jnp.where(west_edge, sides[0], pltpu.roll(potential, 1, 1))
    tall = north - south
    zonal_ref[...] = (east - west) * 0.5
    meridional_ref[...] = tall * 0.5

    for r in range(rows):
        for c in range(blocks):
            lanes = slice(c * TILE, (c + 1) * TILE)
            start = (r * blocks + c) * FIELDS
            place = slice(start, start + FIELDS)
            zonal = jnp.broadcast_to(zonal_ref[r : r + 1, lanes], (FIELDS, TILE))
            meridional = jnp.broadcast_to(meridional_ref[r : r + 1, lanes], (FIELDS, TILE))
            moved_ref[place, :] = (
                still_ref[place, :]
                + zonal * lon_ref[place, :]
                + meridional * lat_ref[place, :]
            )
    zero_tile(moved_ref)
    pack_tiles(lon, place_ref, moved_ref, send_refs)

    small_row = lax.broadcasted_iota(jnp.int32, (rows, TILE), 0)

    def side_tall(column, low, high):
        wide = jnp.broadcast_to(column, (rows, TILE))
        up = jnp.where(small_row == rows - 1, high, pltpu.roll(wide, rows - 1, 0))
        down = jnp.where(small_row == 0, low, pltpu.roll(wide, 1, 0))
        return (up - down)[:, 0:1]

    west_tall = side_tall(sides[0], corners[0], corners[2])
    east_tall = side_tall(sides[1], corners[1], corners[3])
    tall_east = jnp.where(east_edge, east_tall, pltpu.roll(tall, cols - 1, 1))
    tall_west = jnp.where(west_edge, west_tall, pltpu.roll(tall, 1, 1))
    mixed = (tall_east - tall_west) * 0.25
    second_lon = east - 2.0 * potential + west
    second_lat = north - 2.0 * potential + south
    det_ref[...] = (1.0 + second_lon) * (1.0 + second_lat) - mixed * mixed


def last_kernel(n_dev, got_ref, old_ref, monitor_ref, balance_ref, pot_ref, scaled_ref):
    rows, cols = monitor_ref.shape
    target, spread = whole_stats(got_ref, n_dev, rows * cols, 0)
    residual = balance_ref[...] - target
    scaled_ref[...] = residual / spread
    pot_ref[...] = old_ref[...] + 0.5 * residual / (monitor_ref[...] * spread)


def per_device(pq, coef, departing, occupancy, arriving, blocks_w):
    n_lat, n_lon = lax.axis_size("lat"), lax.axis_size("lon")
    n_dev = n_lat * n_lon
    rows, cols = pq.shape[2:]
    ids = departing[0, 0]
    occ = occupancy[0, 0]
    targets = arriving[0, 0]
    weights = blocks_w[0, 0]
    smem = pl.BlockSpec(memory_space=SMEM)
    vmem = pl.BlockSpec(memory_space=VMEM)
    hbm = pl.BlockSpec(memory_space=pltpu.MemorySpace.HBM)
    f32 = jnp.float32
    grid = jax.ShapeDtypeStruct((rows, cols), f32)
    half = n_lon // 2
    tile_rows = FIELDS * rows * cols // TILE
    acc_shape = jax.ShapeDtypeStruct((tile_rows, TILE), f32)
    moved_shape = jax.ShapeDtypeStruct((tile_rows + FIELDS, TILE), f32)
    send_shape = jax.ShapeDtypeStruct((CAP * FIELDS, TILE), jnp.bfloat16)
    half_shape = VMEM((half, CAP, TILE, TILE), weights.dtype)
    params = pltpu.CompilerParams(vmem_limit_bytes=5 << 20)
    early_cost = pl.CostEstimate(
        flops=2 * half * CAP * FIELDS * TILE * TILE,
        bytes_accessed=2 * half * CAP * TILE * TILE,
        transcendentals=0,
    )

    def in_hbm(array):
        return pltpu.with_memory_space_constraint(array, pltpu.MemorySpace.HBM)

    still, places, targets, coef, *send = pl.pallas_call(
        functools.partial(first_kernel, n_lon),
        out_shape=(
            moved_shape,
            jax.ShapeDtypeStruct(ids.shape, ids.dtype),
            jax.ShapeDtypeStruct(targets.shape, targets.dtype),
            jax.ShapeDtypeStruct(coef.shape, coef.dtype),
        )
        + (send_shape,) * n_lon,
        in_specs=[hbm] * 5,
        out_specs=(vmem,) * (4 + n_lon),
        scratch_shapes=[
            pltpu.VMEM(ids.shape, jnp.int32),
            pltpu.SMEM(occ.shape, jnp.int32),
            pltpu.SMEM(ids.shape, jnp.int32),
            pltpu.VMEM(pq.shape[1:], pq.dtype),
            pltpu.SemaphoreType.DMA((5,)),
        ],
        compiler_params=params,
        name="first",
    )(*[in_hbm(x) for x in (ids, occ, targets, coef, pq)])

    def interp(send, moved, det, kept):
        got = list(send)
        for r in range(1, n_lon):
            got[r] = lax.ppermute(send[r], "lon", [(i, i ^ r) for i in range(n_lon)])
        early, late = ([got[r] for r in group] for group in groups(n_lon))
        start_sweep = det is None
        if start_sweep:
            kept = pl.pallas_call(
                functools.partial(fetch_kernel, n_lon),
                out_shape=(half_shape, half_shape, acc_shape, acc_shape),
                in_specs=[hbm] * 2,
                out_specs=(vmem,) * 4,
                scratch_shapes=[
                    pltpu.VMEM((2,) + pq.shape[1:], pq.dtype),
                    pltpu.SemaphoreType.DMA((3,)),
                ],
                compiler_params=params,
                cost_estimate=pl.CostEstimate(
                    flops=1 << 20, bytes_accessed=10 << 20, transcendentals=0
                ),
                name="fetch",
            )(in_hbm(pq), in_hbm(weights))
        base = pl.pallas_call(
            functools.partial(early_kernel, n_lon),
            out_shape=acc_shape,
            in_specs=[smem] + [vmem] * (3 + len(early)),
            out_specs=vmem,
            compiler_params=params,
            cost_estimate=early_cost,
            name="early",
        )(targets, moved, *kept[:2], *early)
        pay_width = TILE + (cols if start_sweep else 2 * cols)
        out_shape = (grid, grid, jax.ShapeDtypeStruct((n_dev, 1, pay_width), f32), acc_shape)
        args = [targets, coef, base, *kept[:2], *late] + ([] if start_sweep else [det])
        outs = pl.pallas_call(
            functools.partial(late_kernel, n_lat, n_lon, start_sweep),
            out_shape=out_shape,
            in_specs=[smem, smem] + [vmem] * (len(args) - 2),
            out_specs=(vmem,) * 4,
            input_output_aliases={2: 3},
            compiler_params=params,
            name="late",
        )(*args)
        outs = outs[:3]
        return (*outs, kept)

    def share(pay):
        return lax.all_to_all(pay, ("lat", "lon"), 0, 0, tiled=True)

    gots = []
    moved = still
    potential = det = kept = None
    for sweep in range(SWEEPS):
        monitor, balance, pay, kept = interp(send, moved, det, kept)
        if sweep == SWEEPS - 1:
            break
        gots.append(share(pay))
        olds = [] if potential is None else [potential]
        args = [places, *gots, *olds, monitor, balance, still, *kept[2:]]
        potential, det, moved, *send = pl.pallas_call(
            functools.partial(update_kernel, n_lat, n_lon, len(gots)),
            out_shape=(grid, grid, moved_shape) + (send_shape,) * n_lon,
            in_specs=[smem] + [vmem] * (len(args) - 1),
            out_specs=(vmem,) * (3 + n_lon),
            scratch_shapes=[pltpu.VMEM((rows, cols), f32)] * 2,
            compiler_params=params,
            name="update",
        )(*args)

    got = share(pay[:, :, pay.shape[2] - TILE :])
    return pl.pallas_call(
        functools.partial(last_kernel, n_dev),
        out_shape=(grid, grid),
        in_specs=[vmem] * 4,
        out_specs=(vmem, vmem),
        compiler_params=params,
        name="last",
    )(got, potential, monitor, balance)


def solution(mesh):
    in_specs = (
        P(None, None, "lat", "lon"),
        P(),
        P("lat", "lon", None, None),
        P("lat", "lon", None),
        P("lat", "lon", None, None),
        P("lat", "lon", None, None, None, None),
    )
    out_specs = (P("lat", "lon"), P("lat", "lon"))
    return jax.shard_map(
        per_device, mesh=mesh, in_specs=in_specs, out_specs=out_specs, check_vma=False
    )
```
